128 devices in a mesh: bond: 8 (over x, core), op: 16 (over y, z).
Axes of the slice: x: 4, y: 4, z: 4, core: 2. Of those that a mesh axis runs over, the one named last changes fastest.
Arguments:
- wave_slab: bfloat16 [8192, 8192], P('op', 'bond'), may hold values from -6 to 6
- left_blocks: bfloat16 [32, 16, 2, 128, 128], P('op'), may hold values from -0.375 to 0.375
- right_blocks: bfloat16 [32, 64, 2, 128, 128], P('op'), may hold values from -0.0625 to 0.0625
- sector_size: int32 [64], replicated, may hold values from 1 to 128
- left_pairs: int32 [32, 16, 2], P('op'), may hold values from 0 to 63
- right_pairs: int32 [32, 64, 2], P('op'), may hold values from 0 to 63
Outputs:
- applied: float32 [2048, 8192], P('bond', 'op')
The draws below stay inside these ranges and needn't reach their ends.
All inputs are finite; a program needn't handle non-finite values.
Results may differ from the reference program's by a relative error of at most 0.0029.
Values may be sent and summed in bfloat16 or wider, within the bound.
No kernel may reach another device: no remote copies, remote signals or barrier semaphores. Data moves between devices by JAX's collectives and lax.ppermute only.
A program may use at most 128 MiB of HBM per device.

```python
import jax
import jax.numpy as jnp
from jax import lax

D = 8192
TILE = 128
NP = 2
RSEC = 16
K = 32
NSEC = 64
RROWS = 2048


def touch_ends(result, key, smallest, largest):
    place = [jax.random.randint(jax.random.fold_in(key, axis), (), 0, length) for axis, length in enumerate(result.shape)]
    main_axis = result.shape.index(max(result.shape))
    neighbour = place[:main_axis] + [(place[main_axis] + 1) % result.shape[main_axis]] + place[main_axis + 1:]
    return result.at[tuple(place)].set(smallest).at[tuple(neighbour)].set(largest)


def levels(key, dims, shards, smallest, high):
    loudness = 1.0
    for position, parts in shards:
        steps = jax.random.uniform(jax.random.fold_in(jax.random.fold_in(key, 6), position), (parts,), jnp.float32, smallest / len(shards), high / len(shards))
        loudness = loudness * jnp.repeat(jnp.exp(steps), dims[position] // parts).reshape((-1,) + (1,) * (len(dims) - 1 - position))
    return loudness


def gaussian(stream_key, extent, width, bound, cuts=(), kind=jnp.bfloat16):
    drawn = jax.random.normal(stream_key, extent, jnp.float32) * width
    if len(cuts) > 0:
        drawn = levels(stream_key, extent, cuts, -0.22, 0.18) * drawn
    return jnp.clip(drawn, min=-bound, max=bound).astype(kind)


def setup_inputs(seed: int = 0) -> dict:
    arg_keys = jax.random.split(jax.random.key(seed), 7)
    wave_slab = gaussian(arg_keys[0], (D, D), 1.0, 6.0, ((0, 16), (1, 8)))
    left_blocks = gaussian(arg_keys[1], (K, RSEC, NP, TILE, TILE), (NP * TILE) ** -0.5, 0.375, ((0, 16),))
    right_blocks = gaussian(arg_keys[2], (K, NSEC, NP, TILE, TILE), (NP * TILE * K) ** -0.5, 0.0625, ((0, 16),))
    sector_size = touch_ends(jax.random.randint(arg_keys[3], (NSEC,), 1, TILE + 1), jax.random.fold_in(arg_keys[3], 1), 1, TILE).astype(jnp.int32)
    left_pairs = touch_ends(jax.random.randint(arg_keys[4], (K, RSEC, NP), 0, NSEC), jax.random.fold_in(arg_keys[4], 1), 0, NSEC - 1).astype(jnp.int32)
    right_pairs = touch_ends(jax.random.randint(arg_keys[5], (K, NSEC, NP), 0, NSEC), jax.random.fold_in(arg_keys[5], 1), 0, NSEC - 1).astype(jnp.int32)
    return {"wave_slab": wave_slab, "left_blocks": left_blocks, "right_blocks": right_blocks, "sector_size": sector_size, "left_pairs": left_pairs, "right_pairs": right_pairs}


def live_mask(sector_size):
    states = jnp.arange(TILE, dtype=jnp.int32)
    return (states[None, :] < sector_size[:, None]).astype(jnp.float32).reshape(-1)


def reference(wave_slab, left_blocks, right_blocks, sector_size, left_pairs, right_pairs):
    live = live_mask(sector_size)
    masked = (wave_slab.astype(jnp.float32) * live[:, None] * live[None, :]).astype(jnp.bfloat16)
    sectors = masked.reshape(NSEC, TILE, D)

    def one_term(total, inputs):
        left_term, right_term, left_sel, right_sel = inputs
        picked = sectors[left_sel]
        middle = jnp.einsum("ipxy,ipyb->ixb", left_term.astype(jnp.float32), picked.astype(jnp.float32))
        middle = middle.astype(jnp.bfloat16).reshape(RROWS, NSEC, TILE)
        chosen = middle[:, right_sel]
        product = jnp.einsum("rjpy,jpyz->rjz", chosen.astype(jnp.float32), right_term.astype(jnp.float32))
        return total + product.reshape(RROWS, D), None

    start = jnp.zeros((RROWS, D), jnp.float32)
    total, _ = lax.scan(one_term, start, (left_blocks, right_blocks, left_pairs, right_pairs))
    return total * live[:RROWS, None] * live[None, :]
```

```python
import functools

import jax
import jax.numpy as jnp
from jax import lax
from jax.experimental import pallas as pl
from jax.experimental.pallas import tpu as pltpu
from jax.sharding import PartitionSpec as P

TILE = 128
SIDE = 4
GROUP = SIDE * SIDE
BF16 = jnp.bfloat16
F32 = jnp.float32
CHUNKS = (256, 256, 256, 256)


def move(value, step_y, step_z):
    pairs = [
        (y * SIDE + z, (y + step_y) % SIDE * SIDE + (z + step_z) % SIDE)
        for y in range(SIDE)
        for z in range(SIDE)
    ]
    return lax.ppermute(value, "op", pairs)


def left_kernel(first_sector, place, pairs, size, *refs):
    pieces, left_hbm, out, whole, left, sems, left_sem = refs[:8], *refs[8:]
    y, z, bond = place[0], place[1], place[2]
    width = whole.shape[2]
    copies = [pltpu.make_async_copy(left_hbm, left, left_sem)]
    for idx, piece in enumerate(pieces):
        far = idx % SIDE
        for near in range(SIDE):
            step_y, step_z = (far, near) if idx < SIDE else (near, far)
            owner = (y + SIDE - step_y) % SIDE * SIDE + (z + SIDE - step_z) % SIDE
            start = owner * 4 + (0 if idx < SIDE else 2)
            copies.append(
                pltpu.make_async_copy(
                    piece.at[near], whole.at[pl.ds(start, 2)], sems.at[idx * SIDE + near]
                )
            )
    for copy in copies:
        copy.start()
    for copy in copies:
        copy.wait()
    lane = lax.broadcasted_iota(jnp.int32, (TILE, TILE), 1)
    strip_sectors = 8
    col_live = jnp.concatenate(
        [
            (lane[:1] < size[bond * strip_sectors + first_sector + s]).astype(F32)
            for s in range(width // TILE)
        ],
        axis=1,
    )
    terms, rows = left.shape[0], left.shape[1]

    @pl.loop(0, terms * rows)
    def _(step):
        term, row = step // rows, step % rows
        low, high = pairs[step * 2], pairs[step * 2 + 1]
        zero = jnp.zeros((TILE, TILE), BF16)
        lhs = jnp.concatenate(
            [
                jnp.where(lane < size[low], left[term, row, 0], zero),
                jnp.where(lane < size[high], left[term, row, 1], zero),
            ],
            axis=1,
        )
        rhs = jnp.concatenate([whole[low], whole[high]], axis=0)
        middle = (jnp.dot(lhs, rhs, preferred_element_type=F32) * col_live).astype(BF16)
        for s in range(width // TILE):
            out[row // 2, s, term, pl.ds(row % 2 * TILE, TILE), :] = middle[
                :, s * TILE : (s + 1) * TILE
            ]


def left_stage(pieces, left_blocks, place, pairs, size, first_sector):
    width = pieces[0].shape[-1]
    terms = left_blocks.shape[0]
    pieces = [piece.reshape(SIDE, 2, TILE, width) for piece in pieces]
    sector_count = width // TILE
    return pl.pallas_call(
        functools.partial(left_kernel, first_sector),
        name=f"left_{first_sector}",
        out_shape=jax.ShapeDtypeStruct((8, sector_count, terms, 2 * TILE, TILE), BF16),
        grid_spec=pltpu.PrefetchScalarGridSpec(
            num_scalar_prefetch=3,
            grid=(1,),
            in_specs=[pl.BlockSpec(memory_space=pl.ANY)] * 9,
            out_specs=pl.BlockSpec(
                (8, sector_count, terms, 2 * TILE, TILE), lambda i, *_: (0, 0, 0, 0, 0)
            ),
            scratch_shapes=[
                pltpu.VMEM((64, TILE, width), BF16),
                pltpu.VMEM(left_blocks.shape, BF16),
                pltpu.SemaphoreType.DMA((32,)),
                pltpu.SemaphoreType.DMA(()),
            ],
        ),
        compiler_params=pltpu.CompilerParams(vmem_limit_bytes=24 << 20),
        cost_estimate=pl.CostEstimate(
            flops=2 * terms * 2048 * 256 * width,
            bytes_accessed=8192 * width * 2 + (2 << 20) + terms * 2048 * width * 2,
            transcendentals=0,
        ),
    )(place, pairs, size, *pieces, left_blocks)


def right_kernel(counts, place, pairs, size, *refs):
    arrived = refs[: len(counts)]
    right = refs[len(counts)]
    outs_a = refs[len(counts) + 1 : len(counts) + 5]
    outs_b = refs[len(counts) + 5 : len(counts) + 9]
    middle, sems = refs[len(counts) + 9 :]
    step_z, step_y = pl.program_id(0), pl.program_id(1)
    bond = place[2]

    @pl.when((step_z == 0) & (step_y == 0))
    def _():
        copies = []
        first = 0
        for chunk, count in zip(arrived, counts):
            for source in range(8):
                copies.append(
                    pltpu.make_async_copy(
                        chunk.at[source],
                        middle.at[pl.ds(source * 8 + first, count)],
                        sems.at[len(copies)],
                    )
                )
            first += count
        for copy in copies:
            copy.start()
        for copy in copies:
            copy.wait()

    owner = (place[0] + step_y) % SIDE * SIDE + (place[1] + step_z) % SIDE
    rows = middle.shape[2]
    terms = middle.shape[1]
    line = lax.broadcasted_iota(jnp.int32, (TILE, TILE), 0)
    lane = lax.broadcasted_iota(jnp.int32, (TILE, TILE), 1)
    row_live = jnp.concatenate([line < size[bond * 2 + h] for h in range(rows // TILE)], axis=0)
    lanes = jnp.concatenate([lane] * (rows // TILE), axis=0)
    results = []
    for q in range(4):
        col = owner * 4 + q
        parts = []
        for term in range(terms):
            for p in range(2):
                parts.append(middle[pairs[(term * 64 + col) * 2 + p], term])
        lhs = jnp.concatenate(parts, axis=1)
        rhs = jnp.concatenate(
            [right[term, q, p] for term in range(terms) for p in range(2)], axis=0
        )
        product = jnp.dot(lhs, rhs, preferred_element_type=F32)
        keep = row_live & (lanes < size[col])
        results.append(jnp.where(keep, product, 0.0).astype(BF16))
    for k in range(SIDE):

        @pl.when(step_z == k)
        def _():
            outs_a[k][0, :, :TILE] = results[0]
            outs_a[k][0, :, TILE:] = results[1]

        @pl.when(step_y == k)
        def _():
            outs_b[k][0, :, :TILE] = results[2]
            outs_b[k][0, :, TILE:] = results[3]


def right_stage(arrived, right_blocks, place, pairs, size):
    counts = tuple(a.shape[1] for a in arrived)
    terms, rows = arrived[0].shape[2], arrived[0].shape[3]

    def right_index(step_z, step_y, place, pairs, size):
        owner = (place[0] + step_y) % SIDE * SIDE + (place[1] + step_z) % SIDE
        return (0, owner, 0, 0, 0)

    def a_index(k):
        return lambda step_z, step_y, *_: (
            jnp.where(step_z == k, step_y, jnp.where(step_z < k, 0, SIDE - 1)),
            0,
            0,
        )

    def b_index(step_z, step_y, *_):
        return (step_z, 0, 0)

    block = (1, rows, 2 * TILE)
    shape = jax.ShapeDtypeStruct((SIDE, rows, 2 * TILE), BF16)
    return pl.pallas_call(
        functools.partial(right_kernel, counts),
        name="right",
        out_shape=[shape] * 8,
        grid_spec=pltpu.PrefetchScalarGridSpec(
            num_scalar_prefetch=3,
            grid=(SIDE, SIDE),
            in_specs=[pl.BlockSpec(memory_space=pl.ANY)] * len(counts)
            + [pl.BlockSpec((terms, 4, 2, TILE, TILE), right_index)],
            out_specs=[pl.BlockSpec(block, a_index(k)) for k in range(SIDE)]
            + [pl.BlockSpec(block, b_index) for k in range(SIDE)],
            scratch_shapes=[
                pltpu.VMEM((64, terms, rows, TILE), BF16),
                pltpu.SemaphoreType.DMA((8 * len(counts),)),
            ],
        ),
        compiler_params=pltpu.CompilerParams(vmem_limit_bytes=32 << 20),
        cost_estimate=pl.CostEstimate(
            flops=2 * terms * rows * 256 * 8192,
            bytes_accessed=(20 << 20),
            transcendentals=0,
        ),
    )(place, pairs, size, *arrived, right_blocks)


def sum_kernel(*refs):
    inputs, outputs = refs[:8], refs[8:]
    for half in range(2):
        mine = inputs[half * 4 : half * 4 + 4]
        total = mine[0][...].astype(F32)
        for other in mine[1:]:
            total = total + other[...].astype(F32)
        kept = outputs[half * 4 : half * 4 + 4]
        kept[0][...] = total[0]
        for k in range(1, SIDE):
            kept[k][...] = total[k].astype(BF16)


def sum_stage(pieces):
    rows, width = pieces[0].shape[1:]
    whole = pl.BlockSpec(memory_space=pltpu.VMEM)
    kinds = [F32, BF16, BF16, BF16]
    return pl.pallas_call(
        sum_kernel,
        name="near_sum",
        out_shape=[jax.ShapeDtypeStruct((rows, width), kind) for kind in kinds * 2],
        in_specs=[whole] * 8,
        out_specs=[whole] * 8,
        compiler_params=pltpu.CompilerParams(vmem_limit_bytes=16 << 20),
    )(*pieces)


def last_kernel(*refs):
    out = refs[8]
    width = refs[0].shape[1]
    for half in range(2):
        mine = refs[half * 4 : half * 4 + 4]
        total = mine[0][...]
        for other in mine[1:]:
            total = total + other[...].astype(F32)
        out[:, half * width : (half + 1) * width] = total


def last_stage(pieces):
    rows, width = pieces[0].shape
    whole = pl.BlockSpec(memory_space=pltpu.VMEM)
    return pl.pallas_call(
        last_kernel,
        name="far_sum",
        out_shape=jax.ShapeDtypeStruct((rows, 2 * width), F32),
        in_specs=[whole] * 8,
        out_specs=whole,
        compiler_params=pltpu.CompilerParams(vmem_limit_bytes=16 << 20),
    )(*pieces)


def on_device(wave_slab, left_blocks, right_blocks, sector_size, left_pairs, right_pairs):
    group = lax.axis_index("op")
    place = jnp.stack([group // SIDE, group % SIDE, lax.axis_index("bond")]).astype(jnp.int32)
    lefts, rights = left_pairs.reshape(-1), right_pairs.reshape(-1)
    half = wave_slab.shape[0] // 2
    arrived = []
    start = 0
    for width in CHUNKS:
        upper = wave_slab[:half, start : start + width]
        lower = wave_slab[half:, start : start + width]
        upper_row = jnp.stack([upper] + [move(upper, 0, d) for d in range(1, SIDE)])
        lower_row = jnp.stack([lower] + [move(lower, d, 0) for d in range(1, SIDE)])
        pieces = [upper_row] + [move(upper_row, d, 0) for d in range(1, SIDE)]
        pieces += [lower_row] + [move(lower_row, 0, d) for d in range(1, SIDE)]
        middle = left_stage(pieces, left_blocks, place, lefts, sector_size, start // TILE)
        arrived.append(lax.all_to_all(middle, "bond", split_axis=0, concat_axis=0, tiled=True))
        start += width
    parts = right_stage(arrived, right_blocks, place, rights, sector_size)
    near = [parts[0]] + [move(parts[d], 0, d) for d in range(1, SIDE)]
    near += [parts[4]] + [move(parts[4 + d], d, 0) for d in range(1, SIDE)]
    sums = sum_stage(near)
    far = [sums[0]] + [move(sums[d], d, 0) for d in range(1, SIDE)]
    far += [sums[4]] + [move(sums[4 + d], 0, d) for d in range(1, SIDE)]
    return last_stage(far)


def solution(mesh):
    placed = (
        P("op", "bond"),
        P("op", None, None, None, None),
        P("op", None, None, None, None),
        P(),
        P("op", None, None),
        P("op", None, None),
    )
    return jax.shard_map(
        on_device, mesh=mesh, in_specs=placed, out_specs=P("bond", "op"), check_vma=False
    )
```

```python
import functools

import jax
import jax.numpy as jnp
from jax import lax
from jax.experimental import pallas as pl
from jax.experimental.pallas import tpu as pltpu
from jax.sharding import PartitionSpec as P


TILE = 128
SIDE = 4
GROUP = SIDE * SIDE
BF16 = jnp.bfloat16
F32 = jnp.float32
CHUNKS = (256, 256, 256, 256)
NEAR_GROUPS = ((0, 1), (2, 3))


def move(value, step_y, step_z):
    pairs = [
        (y * SIDE + z, (y + step_y) % SIDE * SIDE + (z + step_z) % SIDE)
        for y in range(SIDE)
        for z in range(SIDE)
    ]
    return lax.ppermute(value, "op", pairs)


def left_kernel(first_sector, layout, place, pairs, size, *refs):
    pieces = refs[: len(layout)]
    left_hbm, out, whole, left, sems, left_sem = refs[len(layout) :]
    y, z, bond = place[0], place[1], place[2]
    width = whole.shape[2]
    copies = [pltpu.make_async_copy(left_hbm, left, left_sem)]
    for piece, (upper, far, first) in zip(pieces, layout):
        for slot in range(piece.shape[0]):
            near = first + slot
            step_y, step_z = (far, near) if upper else (near, far)
            owner = (y + SIDE - step_y) % SIDE * SIDE + (z + SIDE - step_z) % SIDE
            start = owner * 4 + (0 if upper else 2)
            copies.append(
                pltpu.make_async_copy(
                    piece.at[slot], whole.at[pl.ds(start, 2)], sems.at[len(copies) - 1]
                )
            )
    for copy in copies:
        copy.start()
    for copy in copies:
        copy.wait()
    lane = lax.broadcasted_iota(jnp.int32, (TILE, TILE), 1)
    strip_sectors = 8
    col_live = jnp.concatenate(
        [
            (lane[:1] < size[bond * strip_sectors + first_sector + s]).astype(F32)
            for s in range(width // TILE)
        ],
        axis=1,
    )
    terms, rows = left.shape[0], left.shape[1]
    zero = jnp.zeros((TILE, TILE), BF16)
    unroll = 4

    @pl.loop(0, terms * rows // unroll)
    def _(trip):
        for u in range(unroll):
            step = trip * unroll + u
            term, row = step // rows, step % rows
            low, high = pairs[step * 2], pairs[step * 2 + 1]
            lhs = jnp.concatenate(
                [
                    jnp.where(lane < size[low], left[term, row, 0], zero),
                    jnp.where(lane < size[high], left[term, row, 1], zero),
                ],
                axis=1,
            )
            rhs = jnp.concatenate([whole[low], whole[high]], axis=0)
            middle = (jnp.dot(lhs, rhs, preferred_element_type=F32) * col_live).astype(BF16)
            for s in range(width // TILE):
                out[row // 2, s, term, pl.ds(row % 2 * TILE, TILE), :] = middle[
                    :, s * TILE : (s + 1) * TILE
                ]


def left_stage(pieces, layout, left_blocks, place, pairs, size, first_sector):
    width = pieces[0].shape[-1]
    terms = left_blocks.shape[0]
    sector_count = width // TILE
    return pl.pallas_call(
        functools.partial(left_kernel, first_sector, layout),
        out_shape=jax.ShapeDtypeStruct((8, sector_count, terms, 2 * TILE, TILE), BF16),
        grid_spec=pltpu.PrefetchScalarGridSpec(
            num_scalar_prefetch=3,
            grid=(1,),
            in_specs=[pl.BlockSpec(memory_space=pl.ANY)] * (len(pieces) + 1),
            out_specs=pl.BlockSpec(
                (8, sector_count, terms, 2 * TILE, TILE), lambda i, *_: (0, 0, 0, 0, 0)
            ),
            scratch_shapes=[
                pltpu.VMEM((64, TILE, width), BF16),
                pltpu.VMEM(left_blocks.shape, BF16),
                pltpu.SemaphoreType.DMA((32,)),
                pltpu.SemaphoreType.DMA(()),
            ],
        ),
        compiler_params=pltpu.CompilerParams(vmem_limit_bytes=60 << 20),
        cost_estimate=pl.CostEstimate(
            flops=2 * terms * 2048 * 256 * width,
            bytes_accessed=8192 * width * 2 + (2 << 20) + terms * 2048 * width * 2,
            transcendentals=0,
        ),
    )(place, pairs, size, *pieces, left_blocks)


def right_kernel(counts, place, pairs, size, *refs):
    arrived = refs[: len(counts)]
    right_hbm = refs[len(counts)]
    outs_a = refs[len(counts) + 1 : len(counts) + 5]
    outs_b = refs[len(counts) + 5 : len(counts) + 9]
    middle, right, sum_a, sum_b, sems, right_sems, out_sems = refs[len(counts) + 9 :]
    bond = place[2]
    copies = []
    first = 0
    for chunk, count in zip(arrived, counts):
        for source in range(8):
            copies.append(
                pltpu.make_async_copy(
                    chunk.at[source],
                    middle.at[pl.ds(source * 8 + first, count)],
                    sems.at[len(copies)],
                )
            )
        first += count
    for copy in copies:
        copy.start()

    def owner_of(step_z, step_y):
        return (place[0] + step_y) % SIDE * SIDE + (place[1] + step_z) % SIDE

    def right_copy(step_z, step_y):
        return pltpu.make_async_copy(
            right_hbm.at[:, pl.ds(owner_of(step_z, step_y) * 4, 4)],
            right.at[step_z * SIDE + step_y],
            right_sems.at[step_z * SIDE + step_y],
        )

    for step_z in range(SIDE):
        for step_y in range(SIDE):
            right_copy(step_z, step_y).start()
    rows = middle.shape[2]
    terms = middle.shape[1]
    line = lax.broadcasted_iota(jnp.int32, (TILE, TILE), 0)
    lane = lax.broadcasted_iota(jnp.int32, (TILE, TILE), 1)
    row_live = jnp.concatenate([line < size[bond * 2 + h] for h in range(rows // TILE)], axis=0)
    lanes = jnp.concatenate([lane] * (rows // TILE), axis=0)
    for copy in copies:
        copy.wait()
    sent = []
    for step_z in range(SIDE):

        @pl.loop(0, SIDE)
        def _(step_y):
            right_copy(step_z, step_y).wait()
            owner = owner_of(step_z, step_y)
            blocks = right.at[step_z * SIDE + step_y]
            for q in range(4):
                col = owner * 4 + q
                lhs = jnp.concatenate(
                    [
                        middle[pairs[(term * 64 + col) * 2 + p], term]
                        for term in range(terms)
                        for p in range(2)
                    ],
                    axis=1,
                )
                rhs = jnp.concatenate(
                    [blocks[term, q, p] for term in range(terms) for p in range(2)], axis=0
                )
                product = jnp.dot(lhs, rhs, preferred_element_type=F32)
                keep = row_live & (lanes < size[col])
                value = jnp.where(keep, product, 0.0).astype(BF16)
                if q < 2:
                    sum_a[step_z, step_y, :, q * TILE : (q + 1) * TILE] = value
                else:
                    sum_b[step_y, step_z, :, (q - 2) * TILE : (q - 1) * TILE] = value

        sent.append(
            pltpu.make_async_copy(sum_a.at[step_z], outs_a[step_z], out_sems.at[len(sent)])
        )
        sent[-1].start()
        for k in range(SIDE):
            sent.append(
                pltpu.make_async_copy(
                    sum_b.at[k, step_z], outs_b[k].at[step_z], out_sems.at[len(sent)]
                )
            )
            sent[-1].start()
    for copy in sent:
        copy.wait()


def right_stage(arrived, right_blocks, place, pairs, size):
    counts = tuple(a.shape[1] for a in arrived)
    terms, rows = arrived[0].shape[2], arrived[0].shape[3]
    shape = jax.ShapeDtypeStruct((SIDE, rows, 2 * TILE), BF16)
    anywhere = pl.BlockSpec(memory_space=pl.ANY)
    return pl.pallas_call(
        functools.partial(right_kernel, counts),
        name="right",
        out_shape=[shape] * 8,
        grid_spec=pltpu.PrefetchScalarGridSpec(
            num_scalar_prefetch=3,
            grid=(1,),
            in_specs=[anywhere] * (len(counts) + 1),
            out_specs=[anywhere] * 8,
            scratch_shapes=[
                pltpu.VMEM((64, terms, rows, TILE), BF16),
                pltpu.VMEM((GROUP, terms, 4, 2, TILE, TILE), BF16),
                pltpu.VMEM((SIDE, SIDE, rows, 2 * TILE), BF16),
                pltpu.VMEM((SIDE, SIDE, rows, 2 * TILE), BF16),
                pltpu.SemaphoreType.DMA((8 * len(counts),)),
                pltpu.SemaphoreType.DMA((GROUP,)),
                pltpu.SemaphoreType.DMA((SIDE * (SIDE + 1),)),
            ],
        ),
        compiler_params=pltpu.CompilerParams(vmem_limit_bytes=60 << 20),
        cost_estimate=pl.CostEstimate(
            flops=2 * terms * rows * 256 * 8192,
            bytes_accessed=(20 << 20),
            transcendentals=0,
        ),
    )(place, pairs, size, *arrived, right_blocks)


def sum_kernel(*refs):
    inputs, outputs = refs[:8], refs[8:]
    for half in range(2):
        mine = inputs[half * 4 : half * 4 + 4]
        total = mine[0][...].astype(F32)
        for other in mine[1:]:
            total = total + other[...].astype(F32)
        kept = outputs[half * 4 : half * 4 + 4]
        kept[0][...] = total[0]
        for k in range(1, SIDE):
            kept[k][...] = total[k].astype(BF16)


def sum_stage(pieces):
    rows, width = pieces[0].shape[1:]
    whole = pl.BlockSpec(memory_space=pltpu.VMEM)
    kinds = [F32, BF16, BF16, BF16]
    return pl.pallas_call(
        sum_kernel,
        name="near_sum",
        out_shape=[jax.ShapeDtypeStruct((rows, width), kind) for kind in kinds * 2],
        in_specs=[whole] * 8,
        out_specs=[whole] * 8,
        compiler_params=pltpu.CompilerParams(vmem_limit_bytes=16 << 20),
    )(*pieces)


def last_kernel(*refs):
    out = refs[8]
    width = refs[0].shape[1]
    for half in range(2):
        mine = refs[half * 4 : half * 4 + 4]
        total = mine[0][...]
        for other in mine[1:]:
            total = total + other[...].astype(F32)
        out[:, half * width : (half + 1) * width] = total


def last_stage(pieces):
    rows, width = pieces[0].shape
    whole = pl.BlockSpec(memory_space=pltpu.VMEM)
    return pl.pallas_call(
        last_kernel,
        name="far_sum",
        out_shape=jax.ShapeDtypeStruct((rows, 2 * width), F32),
        in_specs=[whole] * 8,
        out_specs=whole,
        compiler_params=pltpu.CompilerParams(vmem_limit_bytes=16 << 20),
    )(*pieces)


def near_row(value, upper):
    steps = [(0, d) if upper else (d, 0) for d in range(1, SIDE)]
    return [value] + [move(value, *step) for step in steps]


def far_pieces(row, upper, forward):
    def turn(value, d):
        return move(value, d, 0) if upper else move(value, 0, d)

    before, after = turn(row, 1), turn(row, SIDE - 1)
    if not forward:
        opposite = turn(row, 2)
        return [(row, 0, 0), (before, 1, 0), (after, 3, 0), (opposite, 2, 0)]
    half = SIDE // 2
    return [
        (row, 0, 0),
        (before, 1, 0),
        (after, 3, 0),
        (turn(before[:half], 1), 2, 0),
        (turn(after[half:], SIDE - 1), 2, half),
    ]


def apply_slab(wave_slab, left_blocks, right_blocks, sector_size, left_pairs, right_pairs):
    group = lax.axis_index("op")
    place = jnp.stack([group // SIDE, group % SIDE, lax.axis_index("bond")]).astype(jnp.int32)
    lefts, rights = left_pairs.reshape(-1), right_pairs.reshape(-1)
    sectors = wave_slab.reshape(4, TILE, wave_slab.shape[1])
    starts = [sum(CHUNKS[:chunk]) for chunk in range(len(CHUNKS) + 1)]
    rows = {}
    for members in NEAR_GROUPS:
        low, high = starts[members[0]], starts[members[-1] + 1]
        both = [near_row(sectors[:2, :, low:high], True), near_row(sectors[2:, :, low:high], False)]
        for chunk in members:
            part = slice(starts[chunk] - low, starts[chunk + 1] - low)
            rows[chunk] = [jnp.stack([v[:, :, part] for v in side]) for side in both]
    arrived = []
    for chunk in range(len(CHUNKS)):
        pieces, layout = [], []
        for row, upper in zip(rows[chunk], (True, False)):
            for value, far, first in far_pieces(row, upper, chunk > 0):
                pieces.append(value)
                layout.append((upper, far, first))
        middle = left_stage(
            pieces, tuple(layout), left_blocks, place, lefts, sector_size, starts[chunk] // TILE
        )
        arrived.append(
            lax.all_to_all(middle, "bond", split_axis=0, concat_axis=0, tiled=True)
        )
    parts = right_stage(arrived, right_blocks, place, rights, sector_size)
    near = [parts[0]] + [move(parts[d], 0, d) for d in range(1, SIDE)]
    near += [parts[4]] + [move(parts[4 + d], d, 0) for d in range(1, SIDE)]
    sums = sum_stage(near)
    far = [sums[0]] + [move(sums[d], d, 0) for d in range(1, SIDE)]
    far += [sums[4]] + [move(sums[4 + d], 0, d) for d in range(1, SIDE)]
    return last_stage(far)


def solution(mesh):
    placed = (
        P("op", "bond"),
        P("op", None, None, None, None),
        P("op", None, None, None, None),
        P(),
        P("op", None, None),
        P("op", None, None),
    )
    return jax.shard_map(
        apply_slab, mesh=mesh, in_specs=placed, out_specs=P("bond", "op"), check_vma=False
    )
```

```python
import functools

import jax
import jax.numpy as jnp
from jax import lax
from jax.experimental import pallas as pl
from jax.experimental.pallas import tpu as pltpu
from jax.sharding import PartitionSpec as P


TILE = 128
SIDE = 4
GROUP = SIDE * SIDE
BF16 = jnp.bfloat16
F32 = jnp.float32
CHUNKS = (2, 2, 2, 2)


def move(value, step_y, step_z):
    pairs = [
        (y * SIDE + z, (y + step_y) % SIDE * SIDE + (z + step_z) % SIDE)
        for y in range(SIDE)
        for z in range(SIDE)
    ]
    return lax.ppermute(value, "op", pairs)


def pack_kernel(plans, wave, *refs):
    outs, sems = refs[-len(plans) - 1 : -1], refs[-1]
    gots = refs[: -len(plans) - 1]
    copies = []
    for out, plan in zip(outs, plans):
        for slot, (source, side, unit) in enumerate(plan):
            if source is None:
                block = wave.at[2 * side : 2 * side + 2, :, unit * TILE : (unit + 1) * TILE]
            else:
                block = gots[source].at[unit]
            copies.append(pltpu.make_async_copy(block, out.at[slot], sems.at[len(copies)]))
    for copy in copies:
        copy.start()
    for copy in copies:
        copy.wait()


def pack_stage(wave, gots, plans):
    shapes = [(len(plan), 2, TILE, TILE) for plan in plans]
    return pl.pallas_call(
        functools.partial(pack_kernel, plans),
        out_shape=[jax.ShapeDtypeStruct(shape, BF16) for shape in shapes],
        grid_spec=pltpu.PrefetchScalarGridSpec(
            num_scalar_prefetch=0,
            grid=(1,),
            in_specs=[pl.BlockSpec(memory_space=pl.ANY)] * (1 + len(gots)),
            out_specs=[pl.BlockSpec(shape, lambda i: (0, 0, 0, 0)) for shape in shapes],
            scratch_shapes=[pltpu.SemaphoreType.DMA((sum(len(plan) for plan in plans),))],
        ),
        compiler_params=pltpu.CompilerParams(vmem_limit_bytes=8 << 20),
        cost_estimate=pl.CostEstimate(flops=0, bytes_accessed=3 << 20, transcendentals=0),
    )(wave, *gots)


def left_kernel(first_sector, split, place, pairs, size, *refs):
    pieces, left_hbm = refs[:8], refs[8]
    outs = refs[9 : 9 + split]
    whole, left, sems, left_sem = refs[9 + split :]
    y, z, bond = place[0], place[1], place[2]
    count = whole.shape[0]
    copies = [pltpu.make_async_copy(left_hbm, left, left_sem)]
    for idx, piece in enumerate(pieces):
        upper, far = idx < SIDE, idx % SIDE
        for near in range(SIDE):
            step_y, step_z = (far, near) if upper else (near, far)
            owner = (y + SIDE - step_y) % SIDE * SIDE + (z + SIDE - step_z) % SIDE
            start = owner * 4 + (0 if upper else 2)
            copies.append(
                pltpu.make_async_copy(
                    piece.at[pl.ds(near * count, count)],
                    whole.at[:, pl.ds(start, 2)],
                    sems.at[len(copies) - 1],
                )
            )
    for copy in copies:
        copy.start()
    for copy in copies:
        copy.wait()
    lane = lax.broadcasted_iota(jnp.int32, (TILE, TILE), 1)
    strip_sectors = 8
    col_live = jnp.concatenate(
        [
            (lane[:1] < size[bond * strip_sectors + first_sector + s]).astype(F32)
            for s in range(count)
        ],
        axis=1,
    )
    terms, rows = left.shape[0], left.shape[1]
    zero = jnp.zeros((TILE, TILE), BF16)
    unroll = 8

    @pl.loop(0, terms * rows // unroll)
    def _(trip):
        for u in range(unroll):
            step = trip * unroll + u
            term, row = step // rows, step % rows
            low, high = pairs[step * 2], pairs[step * 2 + 1]
            lhs = jnp.concatenate(
                [
                    jnp.where(lane < size[low], left[term, row, 0], zero),
                    jnp.where(lane < size[high], left[term, row, 1], zero),
                ],
                axis=1,
            )
            rhs = jnp.concatenate(
                [
                    jnp.concatenate([whole[s, sector] for s in range(count)], axis=1)
                    for sector in (low, high)
                ],
                axis=0,
            )
            middle = (jnp.dot(lhs, rhs, preferred_element_type=F32) * col_live).astype(BF16)
            for s in range(count):
                value = middle[:, s * TILE : (s + 1) * TILE]
                if split == 1:
                    outs[0][row // 2, s, term, u % 2 * TILE : (u % 2 + 1) * TILE, :] = value
                else:
                    outs[u % 2][row // 2, s, term] = value


def left_stage(pieces, split, count, left_blocks, place, pairs, size, first_sector):
    terms = left_blocks.shape[0]
    shape = (8, count, terms, 2 * TILE // split, TILE)
    return pl.pallas_call(
        functools.partial(left_kernel, first_sector, split),
        out_shape=[jax.ShapeDtypeStruct(shape, BF16)] * split,
        grid_spec=pltpu.PrefetchScalarGridSpec(
            num_scalar_prefetch=3,
            grid=(1,),
            in_specs=[pl.BlockSpec(memory_space=pl.ANY)] * (len(pieces) + 1),
            out_specs=[pl.BlockSpec(shape, lambda i, *_: (0, 0, 0, 0, 0))] * split,
            scratch_shapes=[
                pltpu.VMEM((count, 64, TILE, TILE), BF16),
                pltpu.VMEM(left_blocks.shape, BF16),
                pltpu.SemaphoreType.DMA((32,)),
                pltpu.SemaphoreType.DMA(()),
            ],
        ),
        compiler_params=pltpu.CompilerParams(vmem_limit_bytes=60 << 20),
        cost_estimate=pl.CostEstimate(
            flops=2 * terms * 2048 * 256 * count * TILE,
            bytes_accessed=(2 << 20) + (terms * 2048 + 8192) * count * TILE * 2,
            transcendentals=0,
        ),
    )(place, pairs, size, *pieces, left_blocks)


def right_kernel(counts, half, place, pairs, size, *refs):
    arrived = refs[: len(counts)]
    right_hbm = refs[len(counts)]
    outs_a = refs[len(counts) + 1 : len(counts) + 5]
    outs_b = refs[len(counts) + 5 : len(counts) + 9]
    middle, right, sum_a, sum_b, sems, right_sems, out_sems = refs[len(counts) + 9 :]
    bond = place[2]
    rows, terms = middle.shape[2], middle.shape[1]
    copies = []
    first = 0
    for chunk, count in zip(arrived, counts):
        for source in range(8):
            block = chunk.at[source]
            if chunk.shape[3] != rows:
                block = block.at[:, :, half * rows : (half + 1) * rows]
            copies.append(
                pltpu.make_async_copy(
                    block, middle.at[pl.ds(source * 8 + first, count)], sems.at[len(copies)]
                )
            )
        first += count
    for copy in copies:
        copy.start()

    def owner_of(step_z, step_y):
        return (place[0] + step_y) % SIDE * SIDE + (place[1] + step_z) % SIDE

    def right_copy(step_z, step_y):
        return pltpu.make_async_copy(
            right_hbm.at[:, pl.ds(owner_of(step_z, step_y) * 4, 4)],
            right.at[step_z * SIDE + step_y],
            right_sems.at[step_z * SIDE + step_y],
        )

    for step_z in range(SIDE):
        for step_y in range(SIDE):
            right_copy(step_z, step_y).start()
    line = lax.broadcasted_iota(jnp.int32, (TILE, TILE), 0)
    lane = lax.broadcasted_iota(jnp.int32, (TILE, TILE), 1)
    row_live = line < size[bond * 2 + half]
    for copy in copies:
        copy.wait()
    sent = []
    for step_z in range(SIDE):

        @pl.loop(0, SIDE, step=2)
        def _(pair):
            for step_y in (pair, pair + 1):
                right_copy(step_z, step_y).wait()
            for step_y in (pair, pair + 1):
                owner = owner_of(step_z, step_y)
                blocks = right.at[step_z * SIDE + step_y]
                for q in range(4):
                    col = owner * 4 + q
                    lhs = jnp.concatenate(
                        [
                            middle[pairs[(term * 64 + col) * 2 + p], term]
                            for term in range(terms)
                            for p in range(2)
                        ],
                        axis=1,
                    )
                    rhs = jnp.concatenate(
                        [blocks[term, q, p] for term in range(terms) for p in range(2)], axis=0
                    )
                    product = jnp.dot(lhs, rhs, preferred_element_type=F32)
                    keep = row_live & (lane < size[col])
                    value = jnp.where(keep, product, 0.0).astype(BF16)
                    if q < 2:
                        sum_a[step_z, step_y, :, q * TILE : (q + 1) * TILE] = value
                    else:
                        sum_b[step_y, step_z, :, (q - 2) * TILE : (q - 1) * TILE] = value

        sent.append(
            pltpu.make_async_copy(sum_a.at[step_z], outs_a[step_z], out_sems.at[len(sent)])
        )
        sent[-1].start()
        for k in range(SIDE):
            sent.append(
                pltpu.make_async_copy(
                    sum_b.at[k, step_z], outs_b[k].at[step_z], out_sems.at[len(sent)]
                )
            )
            sent[-1].start()
    for copy in sent:
        copy.wait()


def right_stage(arrived, half, right_blocks, place, pairs, size):
    counts = tuple(a.shape[1] for a in arrived)
    terms, rows = arrived[0].shape[2], TILE
    shape = jax.ShapeDtypeStruct((SIDE, rows, 2 * TILE), BF16)
    anywhere = pl.BlockSpec(memory_space=pl.ANY)
    return pl.pallas_call(
        functools.partial(right_kernel, counts, half),
        out_shape=[shape] * 8,
        grid_spec=pltpu.PrefetchScalarGridSpec(
            num_scalar_prefetch=3,
            grid=(1,),
            in_specs=[anywhere] * (len(counts) + 1),
            out_specs=[anywhere] * 8,
            scratch_shapes=[
                pltpu.VMEM((64, terms, rows, TILE), BF16),
                pltpu.VMEM((GROUP, terms, 4, 2, TILE, TILE), BF16),
                pltpu.VMEM((SIDE, SIDE, rows, 2 * TILE), BF16),
                pltpu.VMEM((SIDE, SIDE, rows, 2 * TILE), BF16),
                pltpu.SemaphoreType.DMA((8 * len(counts),)),
                pltpu.SemaphoreType.DMA((GROUP,)),
                pltpu.SemaphoreType.DMA((SIDE * (SIDE + 1),)),
            ],
        ),
        compiler_params=pltpu.CompilerParams(vmem_limit_bytes=60 << 20),
        cost_estimate=pl.CostEstimate(
            flops=2 * terms * rows * 256 * 8192,
            bytes_accessed=(14 << 20),
            transcendentals=0,
        ),
    )(place, pairs, size, *arrived, right_blocks)


def sum_kernel(*refs):
    inputs, outputs = refs[:8], refs[8:]
    for half in range(2):
        mine = inputs[half * 4 : half * 4 + 4]
        total = mine[0][...].astype(F32)
        for other in mine[1:]:
            total = total + other[...].astype(F32)
        kept = outputs[half * 4 : half * 4 + 4]
        kept[0][...] = total[0]
        for k in range(1, SIDE):
            kept[k][...] = total[k].astype(BF16)


def sum_stage(pieces):
    rows, width = pieces[0].shape[1:]
    whole = pl.BlockSpec(memory_space=pltpu.VMEM)
    kinds = [F32, BF16, BF16, BF16]
    return pl.pallas_call(
        sum_kernel,
        name="near_sum",
        out_shape=[jax.ShapeDtypeStruct((rows, width), kind) for kind in kinds * 2],
        in_specs=[whole] * 8,
        out_specs=[whole] * 8,
        compiler_params=pltpu.CompilerParams(vmem_limit_bytes=16 << 20),
    )(*pieces)


def last_kernel(*refs):
    out = refs[-1]
    rows, width = refs[0].shape
    for block in range(len(refs) // SIDE):
        mine = refs[block * 4 : block * 4 + 4]
        total = mine[0][...]
        for other in mine[1:]:
            total = total + other[...].astype(F32)
        line, col = block // 2 * rows, block % 2 * width
        out[line : line + rows, col : col + width] = total


def last_stage(pieces):
    rows, width = pieces[0].shape
    whole = pl.BlockSpec(memory_space=pltpu.VMEM)
    return pl.pallas_call(
        last_kernel,
        name="far_sum",
        out_shape=jax.ShapeDtypeStruct((rows * len(pieces) // 8, 2 * width), F32),
        in_specs=[whole] * len(pieces),
        out_specs=whole,
        compiler_params=pltpu.CompilerParams(vmem_limit_bytes=16 << 20),
    )(*pieces)


def turn(value, d, along_y):
    return move(value, d, 0) if along_y else move(value, 0, d)


def apply_slab(wave_slab, left_blocks, right_blocks, sector_size, left_pairs, right_pairs):
    group = lax.axis_index("op")
    place = jnp.stack([group // SIDE, group % SIDE, lax.axis_index("bond")]).astype(jnp.int32)
    lefts, rights = left_pairs.reshape(-1), right_pairs.reshape(-1)
    chunk_count = len(CHUNKS)
    starts = [sum(CHUNKS[:chunk]) for chunk in range(chunk_count + 1)]
    wave = wave_slab.reshape(4, TILE, wave_slab.shape[1])
    ahead = min(2, chunk_count)

    def sent_both(values, y_first):
        return [
            [value] + [turn(value, d, (side == 0) == y_first) for d in range(1, SIDE)]
            for side, value in enumerate(values)
        ]

    units = range(starts[ahead])
    values = pack_stage(wave, [], [[(None, side, unit) for unit in units] for side in range(2)])
    got = sent_both(values, False)
    near = {chunk: ([got[0][1:], got[1][1:]], starts[chunk]) for chunk in range(ahead)}
    arrived = []
    for chunk in range(chunk_count):
        count = CHUNKS[chunk]
        after = chunk + ahead
        sources, offset = near[chunk]
        plans = []
        for side in range(2):
            plan = [(None, side, starts[chunk] + unit) for unit in range(count)]
            for d in range(SIDE - 1):
                plan += [(side * 3 + d, side, offset + unit) for unit in range(count)]
            if after < chunk_count:
                plan += [(None, 1 - side, starts[after] + unit) for unit in range(CHUNKS[after])]
            plans.append(plan)
        values = pack_stage(wave, sources[0] + sources[1], plans)
        got = sent_both(values, True)
        pieces = got[0] + got[1]
        if after < chunk_count:
            near[after] = ([got[1][1:], got[0][1:]], 4 * count)
        split = 2 if chunk == chunk_count - 1 else 1
        middles = left_stage(
            pieces, split, count, left_blocks, place, lefts, sector_size, starts[chunk]
        )
        for middle in middles:
            arrived.append(lax.all_to_all(middle, "bond", split_axis=0, concat_axis=0, tiled=True))
    finals = []
    for half in range(2):
        mine = arrived[: chunk_count - 1] + [arrived[chunk_count - 1 + half]]
        parts = right_stage(mine, half, right_blocks, place, rights, sector_size)
        got = [parts[0]] + [move(parts[d], 0, d) for d in range(1, SIDE)]
        got += [parts[4]] + [move(parts[4 + d], d, 0) for d in range(1, SIDE)]
        sums = sum_stage(got)
        finals += [sums[0]] + [move(sums[d], d, 0) for d in range(1, SIDE)]
        finals += [sums[4]] + [move(sums[4 + d], 0, d) for d in range(1, SIDE)]
    return last_stage(finals)


def solution(mesh):
    placed = (
        P("op", "bond"),
        P("op", None, None, None, None),
        P("op", None, None, None, None),
        P(),
        P("op", None, None),
        P("op", None, None),
    )
    return jax.shard_map(
        apply_slab, mesh=mesh, in_specs=placed, out_specs=P("bond", "op"), check_vma=False
    )
```

```python
import functools

import jax
import jax.numpy as jnp
from jax import lax
from jax.experimental import pallas as pl
from jax.experimental.pallas import tpu as pltpu
from jax.sharding import PartitionSpec as P


TILE = 128
SIDE = 4
GROUP = SIDE * SIDE
BF16 = jnp.bfloat16
F32 = jnp.float32
CHUNKS = (2, 2, 2, 2)
MODES = ((False,), (True,), (False,), (True, False))


def move(value, step_y, step_z):
    pairs = [
        (y * SIDE + z, (y + step_y) % SIDE * SIDE + (z + step_z) % SIDE)
        for y in range(SIDE)
        for z in range(SIDE)
    ]
    return lax.ppermute(value, "op", pairs)


def pack_kernel(plans, wave, *refs):
    outs, sems = refs[-len(plans) - 1 : -1], refs[-1]
    gots = refs[: -len(plans) - 1]
    copies = []
    for out, plan in zip(outs, plans):
        for slot, (source, side, unit) in enumerate(plan):
            if source is None:
                block = wave.at[2 * side : 2 * side + 2, :, unit * TILE : (unit + 1) * TILE]
            else:
                block = gots[source].at[unit]
            copies.append(pltpu.make_async_copy(block, out.at[slot], sems.at[len(copies)]))
    for copy in copies:
        copy.start()
    for copy in copies:
        copy.wait()


def pack_stage(wave, gots, plans):
    shapes = [(len(plan), 2, TILE, TILE) for plan in plans]
    return pl.pallas_call(
        functools.partial(pack_kernel, plans),
        out_shape=[jax.ShapeDtypeStruct(shape, BF16) for shape in shapes],
        grid_spec=pltpu.PrefetchScalarGridSpec(
            num_scalar_prefetch=0,
            grid=(1,),
            in_specs=[pl.BlockSpec(memory_space=pl.ANY)] * (1 + len(gots)),
            out_specs=[pl.BlockSpec(shape, lambda i: (0, 0, 0, 0)) for shape in shapes],
            scratch_shapes=[pltpu.SemaphoreType.DMA((sum(len(plan) for plan in plans),))],
        ),
        compiler_params=pltpu.CompilerParams(vmem_limit_bytes=8 << 20),
        cost_estimate=pl.CostEstimate(flops=0, bytes_accessed=3 << 20, transcendentals=0),
    )(wave, *gots)


def left_kernel(first_sector, modes, place, pairs, size, *refs):
    split = len(modes)
    pieces, left_hbm = refs[:8], refs[8]
    outs = list(refs[9:-5])
    whole, left, done, sems, left_sem = refs[-5:]
    y, z, bond = place[0], place[1], place[2]
    count = whole.shape[0]
    copies = [pltpu.make_async_copy(left_hbm, left, left_sem)]
    for idx, piece in enumerate(pieces):
        upper, far = idx < SIDE, idx % SIDE
        for near in range(SIDE):
            step_y, step_z = (far, near) if upper else (near, far)
            owner = (y + SIDE - step_y) % SIDE * SIDE + (z + SIDE - step_z) % SIDE
            start = owner * 4 + (0 if upper else 2)
            copies.append(
                pltpu.make_async_copy(
                    piece.at[pl.ds(near * count, count)],
                    whole.at[:, pl.ds(start, 2)],
                    sems.at[len(copies) - 1],
                )
            )
    for copy in copies:
        copy.start()
    for copy in copies:
        copy.wait()
    lane = lax.broadcasted_iota(jnp.int32, (TILE, TILE), 1)
    strip_sectors = 8
    col_live = jnp.concatenate(
        [
            (lane[:1] < size[bond * strip_sectors + first_sector + s]).astype(F32)
            for s in range(count)
        ],
        axis=1,
    )
    terms, rows = left.shape[0], left.shape[1]
    zero = jnp.zeros((TILE, TILE), BF16)
    unroll = 8

    @pl.loop(0, terms * rows // unroll)
    def _(trip):
        for u in range(unroll):
            step = trip * unroll + u
            term, row = step // rows, step % rows
            low, high = pairs[step * 2], pairs[step * 2 + 1]
            lhs = jnp.concatenate(
                [
                    jnp.where(lane < size[low], left[term, row, 0], zero),
                    jnp.where(lane < size[high], left[term, row, 1], zero),
                ],
                axis=1,
            )
            rhs = jnp.concatenate(
                [
                    jnp.concatenate([whole[s, sector] for s in range(count)], axis=1)
                    for sector in (low, high)
                ],
                axis=0,
            )
            middle = (jnp.dot(lhs, rhs, preferred_element_type=F32) * col_live).astype(BF16)
            target = row // 2
            if modes[u % 2 % split]:
                target = (target // 2 + SIDE - bond // 2) % SIDE * 2 + (target + bond) % 2
            half, line = (0, u % 2 * TILE) if split == 1 else (u % 2, 0)
            for s in range(count):
                done[half, target, s, term, line : line + TILE, :] = middle[
                    :, s * TILE : (s + 1) * TILE
                ]

    sent = []
    for half, turned in enumerate(modes):
        for block in range(8):
            out = outs.pop(0) if turned else outs[0].at[block]
            sent.append(pltpu.make_async_copy(done.at[half, block], out, sems.at[len(sent)]))
        if not turned:
            outs.pop(0)
    for copy in sent:
        copy.start()
    for copy in sent:
        copy.wait()


def left_stage(pieces, modes, count, left_blocks, place, pairs, size, first_sector):
    terms = left_blocks.shape[0]
    block = (count, terms, 2 * TILE // len(modes), TILE)
    shapes = []
    for turned in modes:
        shapes += [block] * 8 if turned else [(8, *block)]
    anywhere = pl.BlockSpec(memory_space=pl.ANY)
    results = pl.pallas_call(
        functools.partial(left_kernel, first_sector, modes),
        out_shape=[jax.ShapeDtypeStruct(shape, BF16) for shape in shapes],
        grid_spec=pltpu.PrefetchScalarGridSpec(
            num_scalar_prefetch=3,
            grid=(1,),
            in_specs=[anywhere] * (len(pieces) + 1),
            out_specs=[anywhere] * len(shapes),
            scratch_shapes=[
                pltpu.VMEM((count, 64, TILE, TILE), BF16),
                pltpu.VMEM(left_blocks.shape, BF16),
                pltpu.VMEM((len(modes), 8, *block), BF16),
                pltpu.SemaphoreType.DMA((32,)),
                pltpu.SemaphoreType.DMA(()),
            ],
        ),
        compiler_params=pltpu.CompilerParams(vmem_limit_bytes=60 << 20),
        cost_estimate=pl.CostEstimate(
            flops=2 * terms * 2048 * 256 * count * TILE,
            bytes_accessed=(2 << 20) + (terms * 2048 + 8192) * count * TILE * 2,
            transcendentals=0,
        ),
    )(place, pairs, size, *pieces, left_blocks)
    results = list(results)
    grouped = []
    for turned in modes:
        grouped.append([results.pop(0) for _ in range(8 if turned else 1)])
    return grouped


def exchange(blocks):
    if len(blocks) == 1:
        return [lax.all_to_all(blocks[0], "bond", split_axis=0, concat_axis=0, tiled=True)]
    got = [blocks[0]]
    for turned in range(1, 8):
        step_x, step_core = turned // 2, turned % 2
        pairs = [
            (x * 2 + core, (x + step_x) % SIDE * 2 + (core + step_core) % 2)
            for x in range(SIDE)
            for core in range(2)
        ]
        got.append(lax.ppermute(blocks[turned], "bond", pairs))
    return got


def right_kernel(layout, half, place, pairs, size, *refs):
    total = sum(8 if turned else 1 for _, turned in layout)
    arrived, right = list(refs[:total]), refs[total]
    outs_a, outs_b = refs[total + 1 : total + 5], refs[total + 5 : total + 9]
    middle, blocks, sum_a, sum_b, sems, right_sems, out_sems = refs[total + 9 :]
    bond = place[2]
    rows, terms = middle.shape[2], middle.shape[1]
    copies = []
    first = 0
    for count, turned in layout:
        whole = None if turned else arrived.pop(0)
        for block in range(8):
            source = block
            piece = arrived.pop(0) if turned else whole.at[block]
            if turned:
                source = (bond // 2 + SIDE - block // 2) % SIDE * 2 + (bond + block) % 2
            if piece.shape[2] != rows:
                piece = piece.at[:, :, half * rows : (half + 1) * rows]
            copies.append(
                pltpu.make_async_copy(
                    piece, middle.at[pl.ds(source * 8 + first, count)], sems.at[len(copies)]
                )
            )
        first += count
    for copy in copies:
        copy.start()

    def owner_of(step_z, step_y):
        return (place[0] + step_y) % SIDE * SIDE + (place[1] + step_z) % SIDE

    def right_copy(step_z, step_y):
        return pltpu.make_async_copy(
            right.at[:, pl.ds(owner_of(step_z, step_y) * 4, 4)],
            blocks.at[step_z * SIDE + step_y],
            right_sems.at[step_z * SIDE + step_y],
        )

    for step_y in range(SIDE):
        right_copy(0, step_y).start()
    line = lax.broadcasted_iota(jnp.int32, (TILE, TILE), 0)
    lane = lax.broadcasted_iota(jnp.int32, (TILE, TILE), 1)
    row_live = line < size[bond * 2 + half]
    for copy in copies:
        copy.wait()
    for step_z in range(1, SIDE):
        for step_y in range(SIDE):
            right_copy(step_z, step_y).start()
    sent = []
    for step_z in range(SIDE):

        @pl.loop(0, SIDE, step=2)
        def _(pair):
            for step_y in (pair, pair + 1):
                right_copy(step_z, step_y).wait()
            for step_y in (pair, pair + 1):
                owner = owner_of(step_z, step_y)
                block = blocks.at[step_z * SIDE + step_y]
                for q in range(4):
                    col = owner * 4 + q
                    lhs = jnp.concatenate(
                        [
                            middle[pairs[(term * 64 + col) * 2 + p], term]
                            for term in range(terms)
                            for p in range(2)
                        ],
                        axis=1,
                    )
                    rhs = jnp.concatenate(
                        [block[term, q, p] for term in range(terms) for p in range(2)], axis=0
                    )
                    product = jnp.dot(lhs, rhs, preferred_element_type=F32)
                    keep = row_live & (lane < size[col])
                    value = jnp.where(keep, product, 0.0).astype(BF16)
                    if q < 2:
                        sum_a[step_z, step_y, :, q * TILE : (q + 1) * TILE] = value
                    else:
                        sum_b[step_y, step_z, :, (q - 2) * TILE : (q - 1) * TILE] = value

        sent.append(
            pltpu.make_async_copy(sum_a.at[step_z], outs_a[step_z], out_sems.at[len(sent)])
        )
        sent[-1].start()
        for k in range(SIDE):
            sent.append(
                pltpu.make_async_copy(
                    sum_b.at[k, step_z], outs_b[k].at[step_z], out_sems.at[len(sent)]
                )
            )
            sent[-1].start()
    for copy in sent:
        copy.wait()


def right_stage(arrived, half, right_blocks, place, pairs, size):
    layout = tuple((count, len(blocks) > 1) for count, blocks in zip(CHUNKS, arrived))
    arrived = [block for blocks in arrived for block in blocks]
    terms, rows = right_blocks.shape[0], TILE
    shape = jax.ShapeDtypeStruct((SIDE, rows, 2 * TILE), BF16)
    anywhere = pl.BlockSpec(memory_space=pl.ANY)
    return pl.pallas_call(
        functools.partial(right_kernel, layout, half),
        out_shape=[shape] * 8,
        grid_spec=pltpu.PrefetchScalarGridSpec(
            num_scalar_prefetch=3,
            grid=(1,),
            in_specs=[anywhere] * (len(arrived) + 1),
            out_specs=[anywhere] * 8,
            scratch_shapes=[
                pltpu.VMEM((64, terms, rows, TILE), BF16),
                pltpu.VMEM((GROUP, terms, 4, 2, TILE, TILE), BF16),
                pltpu.VMEM((SIDE, SIDE, rows, 2 * TILE), BF16),
                pltpu.VMEM((SIDE, SIDE, rows, 2 * TILE), BF16),
                pltpu.SemaphoreType.DMA((8 * len(layout),)),
                pltpu.SemaphoreType.DMA((GROUP,)),
                pltpu.SemaphoreType.DMA((SIDE * (SIDE + 1),)),
            ],
        ),
        compiler_params=pltpu.CompilerParams(vmem_limit_bytes=58 << 20),
        cost_estimate=pl.CostEstimate(
            flops=2 * terms * rows * 256 * 8192,
            bytes_accessed=(14 << 20),
            transcendentals=0,
        ),
    )(place, pairs, size, *arrived, right_blocks)


def sum_kernel(*refs):
    inputs, outputs = refs[:8], refs[8:]
    for half in range(2):
        mine = inputs[half * 4 : half * 4 + 4]
        total = mine[0][...].astype(F32)
        for other in mine[1:]:
            total = total + other[...].astype(F32)
        kept = outputs[half * 4 : half * 4 + 4]
        kept[0][...] = total[0]
        for k in range(1, SIDE):
            kept[k][...] = total[k].astype(BF16)


def sum_stage(pieces):
    rows, width = pieces[0].shape[1:]
    whole = pl.BlockSpec(memory_space=pltpu.VMEM)
    kinds = [F32, BF16, BF16, BF16]
    return pl.pallas_call(
        sum_kernel,
        name="near_sum",
        out_shape=[jax.ShapeDtypeStruct((rows, width), kind) for kind in kinds * 2],
        in_specs=[whole] * 8,
        out_specs=[whole] * 8,
        compiler_params=pltpu.CompilerParams(vmem_limit_bytes=16 << 20),
    )(*pieces)


def last_kernel(*refs):
    out = refs[-1]
    rows, width = refs[0].shape
    for block in range(len(refs) // SIDE):
        mine = refs[block * 4 : block * 4 + 4]
        total = mine[0][...]
        for other in mine[1:]:
            total = total + other[...].astype(F32)
        line, col = block // 2 * rows, block % 2 * width
        out[line : line + rows, col : col + width] = total


def last_stage(pieces):
    rows, width = pieces[0].shape
    whole = pl.BlockSpec(memory_space=pltpu.VMEM)
    return pl.pallas_call(
        last_kernel,
        name="far_sum",
        out_shape=jax.ShapeDtypeStruct((rows * len(pieces) // 8, 2 * width), F32),
        in_specs=[whole] * len(pieces),
        out_specs=whole,
        compiler_params=pltpu.CompilerParams(vmem_limit_bytes=16 << 20),
    )(*pieces)


def turn(value, d, along_y):
    return move(value, d, 0) if along_y else move(value, 0, d)


def apply_slab(wave_slab, left_blocks, right_blocks, sector_size, left_pairs, right_pairs):
    group = lax.axis_index("op")
    place = jnp.stack([group // SIDE, group % SIDE, lax.axis_index("bond")]).astype(jnp.int32)
    lefts, rights = left_pairs.reshape(-1), right_pairs.reshape(-1)
    chunk_count = len(CHUNKS)
    starts = [sum(CHUNKS[:chunk]) for chunk in range(chunk_count + 1)]
    wave = wave_slab.reshape(4, TILE, wave_slab.shape[1])
    ahead = min(2, chunk_count)

    def sent_both(values, y_first):
        return [
            [value] + [turn(value, d, (side == 0) == y_first) for d in range(1, SIDE)]
            for side, value in enumerate(values)
        ]

    units = range(starts[ahead])
    values = pack_stage(wave, [], [[(None, side, unit) for unit in units] for side in range(2)])
    got = sent_both(values, False)
    near = {chunk: ([got[0][1:], got[1][1:]], starts[chunk]) for chunk in range(ahead)}
    arrived = []
    for chunk in range(chunk_count):
        count = CHUNKS[chunk]
        after = chunk + ahead
        sources, offset = near[chunk]
        plans = []
        for side in range(2):
            plan = [(None, side, starts[chunk] + unit) for unit in range(count)]
            for d in range(SIDE - 1):
                plan += [(side * 3 + d, side, offset + unit) for unit in range(count)]
            if after < chunk_count:
                plan += [(None, 1 - side, starts[after] + unit) for unit in range(CHUNKS[after])]
            plans.append(plan)
        values = pack_stage(wave, sources[0] + sources[1], plans)
        got = sent_both(values, True)
        pieces = got[0] + got[1]
        if after < chunk_count:
            near[after] = ([got[1][1:], got[0][1:]], 4 * count)
        middles = left_stage(
            pieces, MODES[chunk], count, left_blocks, place, lefts, sector_size, starts[chunk]
        )
        for middle in middles:
            arrived.append(exchange(middle))
    finals = []
    for half in range(2):
        mine = arrived[: chunk_count - 1] + [arrived[chunk_count - 1 + half]]
        parts = right_stage(mine, half, right_blocks, place, rights, sector_size)
        got = [parts[0]] + [move(parts[d], 0, d) for d in range(1, SIDE)]
        got += [parts[4]] + [move(parts[4 + d], d, 0) for d in range(1, SIDE)]
        sums = sum_stage(got)
        finals += [sums[0]] + [move(sums[d], d, 0) for d in range(1, SIDE)]
        finals += [sums[4]] + [move(sums[4 + d], 0, d) for d in range(1, SIDE)]
    return last_stage(finals)


def solution(mesh):
    placed = (
        P("op", "bond"),
        P("op", None, None, None, None),
        P("op", None, None, None, None),
        P(),
        P("op", None, None),
        P("op", None, None),
    )
    return jax.shard_map(
        apply_slab, mesh=mesh, in_specs=placed, out_specs=P("bond", "op"), check_vma=False
    )
```

```python
import functools

import jax
import jax.numpy as jnp
from jax import lax
from jax.experimental import pallas as pl
from jax.experimental.pallas import tpu as pltpu
from jax.sharding import PartitionSpec as P


TILE = 128
SIDE = 4
GROUP = SIDE * SIDE
BF16 = jnp.bfloat16
F32 = jnp.float32
CHUNKS = (2, 2, 2, 2)
MODES = ((False,), (True,), (False,), (True, False))


def move(value, step_y, step_z):
    pairs = [
        (y * SIDE + z, (y + step_y) % SIDE * SIDE + (z + step_z) % SIDE)
        for y in range(SIDE)
        for z in range(SIDE)
    ]
    return lax.ppermute(value, "op", pairs)


def pack_kernel(plans, wave, *refs):
    outs, sems = refs[-len(plans) - 1 : -1], refs[-1]
    gots = refs[: -len(plans) - 1]
    copies = []
    for out, plan in zip(outs, plans):
        for slot, (source, side, unit) in enumerate(plan):
            if source is None:
                block = wave.at[2 * side : 2 * side + 2, :, unit * TILE : (unit + 1) * TILE]
            else:
                block = gots[source].at[unit]
            copies.append(pltpu.make_async_copy(block, out.at[slot], sems.at[len(copies)]))
    for copy in copies:
        copy.start()
    for copy in copies:
        copy.wait()


def pack_stage(wave, gots, plans):
    shapes = [(len(plan), 2, TILE, TILE) for plan in plans]
    return pl.pallas_call(
        functools.partial(pack_kernel, plans),
        out_shape=[jax.ShapeDtypeStruct(shape, BF16) for shape in shapes],
        grid_spec=pltpu.PrefetchScalarGridSpec(
            num_scalar_prefetch=0,
            grid=(1,),
            in_specs=[pl.BlockSpec(memory_space=pl.ANY)] * (1 + len(gots)),
            out_specs=[pl.BlockSpec(shape, lambda i: (0, 0, 0, 0)) for shape in shapes],
            scratch_shapes=[pltpu.SemaphoreType.DMA((sum(len(plan) for plan in plans),))],
        ),
        compiler_params=pltpu.CompilerParams(vmem_limit_bytes=8 << 20),
        cost_estimate=pl.CostEstimate(flops=0, bytes_accessed=3 << 20, transcendentals=0),
    )(wave, *gots)


def left_kernel(first_sector, modes, plan, place, pairs, size, *refs):
    split = len(modes)
    total = 1 + max(entry[0] for entry in plan)
    pieces, left_hbm = refs[:total], refs[total]
    outs = list(refs[total + 1 : -5])
    whole, left, done, sems, left_sem = refs[-5:]
    y, z, bond = place[0], place[1], place[2]
    count = whole.shape[0]
    copies = [pltpu.make_async_copy(left_hbm, left, left_sem)]
    for source, offset, side, far, near in plan:
        step_y, step_z = (far, near) if side == 0 else (near, far)
        owner = (y + SIDE - step_y) % SIDE * SIDE + (z + SIDE - step_z) % SIDE
        copies.append(
            pltpu.make_async_copy(
                pieces[source].at[offset : offset + count],
                whole.at[:, pl.ds(owner * 4 + 2 * side, 2)],
                sems.at[len(copies) - 1],
            )
        )
    for copy in copies:
        copy.start()
    for copy in copies:
        copy.wait()
    lane = lax.broadcasted_iota(jnp.int32, (TILE, TILE), 1)
    strip_sectors = 8
    col_live = jnp.concatenate(
        [
            (lane[:1] < size[bond * strip_sectors + first_sector + s]).astype(F32)
            for s in range(count)
        ],
        axis=1,
    )
    terms, rows = left.shape[0], left.shape[1]
    zero = jnp.zeros((TILE, TILE), BF16)
    unroll = 8

    @pl.loop(0, terms * rows // unroll)
    def _(trip):
        for u in range(unroll):
            step = trip * unroll + u
            term, row = step // rows, step % rows
            low, high = pairs[step * 2], pairs[step * 2 + 1]
            lhs = jnp.concatenate(
                [
                    jnp.where(lane < size[low], left[term, row, 0], zero),
                    jnp.where(lane < size[high], left[term, row, 1], zero),
                ],
                axis=1,
            )
            rhs = jnp.concatenate(
                [
                    jnp.concatenate([whole[s, sector] for s in range(count)], axis=1)
                    for sector in (low, high)
                ],
                axis=0,
            )
            middle = (jnp.dot(lhs, rhs, preferred_element_type=F32) * col_live).astype(BF16)
            target = row // 2
            if modes[u % 2 % split]:
                target = (target // 2 + SIDE - bond // 2) % SIDE * 2 + (target + bond) % 2
            half, line = (0, u % 2 * TILE) if split == 1 else (u % 2, 0)
            for s in range(count):
                done[half, target, s, term, line : line + TILE, :] = middle[
                    :, s * TILE : (s + 1) * TILE
                ]

    sent = []
    for half, turned in enumerate(modes):
        for block in range(8):
            out = outs.pop(0) if turned else outs[0].at[block]
            sent.append(pltpu.make_async_copy(done.at[half, block], out, sems.at[len(sent)]))
        if not turned:
            outs.pop(0)
    for copy in sent:
        copy.start()
    for copy in sent:
        copy.wait()


def left_stage(pieces, plan, modes, count, left_blocks, place, pairs, size, first_sector):
    terms = left_blocks.shape[0]
    block = (count, terms, 2 * TILE // len(modes), TILE)
    shapes = []
    for turned in modes:
        shapes += [block] * 8 if turned else [(8, *block)]
    anywhere = pl.BlockSpec(memory_space=pl.ANY)
    results = pl.pallas_call(
        functools.partial(left_kernel, first_sector, modes, plan),
        out_shape=[jax.ShapeDtypeStruct(shape, BF16) for shape in shapes],
        grid_spec=pltpu.PrefetchScalarGridSpec(
            num_scalar_prefetch=3,
            grid=(1,),
            in_specs=[anywhere] * (len(pieces) + 1),
            out_specs=[anywhere] * len(shapes),
            scratch_shapes=[
                pltpu.VMEM((count, 64, TILE, TILE), BF16),
                pltpu.VMEM(left_blocks.shape, BF16),
                pltpu.VMEM((len(modes), 8, *block), BF16),
                pltpu.SemaphoreType.DMA((32,)),
                pltpu.SemaphoreType.DMA(()),
            ],
        ),
        compiler_params=pltpu.CompilerParams(vmem_limit_bytes=60 << 20),
        cost_estimate=pl.CostEstimate(
            flops=2 * terms * 2048 * 256 * count * TILE,
            bytes_accessed=(2 << 20) + (terms * 2048 + 8192) * count * TILE * 2,
            transcendentals=0,
        ),
    )(place, pairs, size, *pieces, left_blocks)
    results = list(results)
    grouped = []
    for turned in modes:
        grouped.append([results.pop(0) for _ in range(8 if turned else 1)])
    return grouped


def exchange(blocks):
    if len(blocks) == 1:
        return [lax.all_to_all(blocks[0], "bond", split_axis=0, concat_axis=0, tiled=True)]
    got = [blocks[0]]
    for turned in range(1, 8):
        step_x, step_core = turned // 2, turned % 2
        pairs = [
            (x * 2 + core, (x + step_x) % SIDE * 2 + (core + step_core) % 2)
            for x in range(SIDE)
            for core in range(2)
        ]
        got.append(lax.ppermute(blocks[turned], "bond", pairs))
    return got


def right_kernel(layout, half, place, pairs, size, *refs):
    total = sum(8 if turned else 1 for _, turned in layout)
    arrived, right = list(refs[:total]), refs[total]
    outs_a, outs_b = refs[total + 1 : total + 5], refs[total + 5 : total + 9]
    middle, blocks, sum_a, sum_b, sems, right_sems, out_sems = refs[total + 9 :]
    bond = place[2]
    rows, terms = middle.shape[2], middle.shape[1]
    copies = []
    first = 0
    for count, turned in layout:
        whole = None if turned else arrived.pop(0)
        for block in range(8):
            source = block
            piece = arrived.pop(0) if turned else whole.at[block]
            if turned:
                source = (bond // 2 + SIDE - block // 2) % SIDE * 2 + (bond + block) % 2
            if piece.shape[2] != rows:
                piece = piece.at[:, :, half * rows : (half + 1) * rows]
            copies.append(
                pltpu.make_async_copy(
                    piece, middle.at[pl.ds(source * 8 + first, count)], sems.at[len(copies)]
                )
            )
        first += count
    for copy in copies:
        copy.start()

    def owner_of(step_z, step_y):
        return (place[0] + step_y) % SIDE * SIDE + (place[1] + step_z) % SIDE

    def right_copy(step_z, step_y):
        return pltpu.make_async_copy(
            right.at[:, pl.ds(owner_of(step_z, step_y) * 4, 4)],
            blocks.at[step_z * SIDE + step_y],
            right_sems.at[step_z * SIDE + step_y],
        )

    for step_y in range(SIDE):
        right_copy(0, step_y).start()
    line = lax.broadcasted_iota(jnp.int32, (TILE, TILE), 0)
    lane = lax.broadcasted_iota(jnp.int32, (TILE, TILE), 1)
    row_live = line < size[bond * 2 + half]
    for copy in copies:
        copy.wait()
    for step_z in range(1, SIDE):
        for step_y in range(SIDE):
            right_copy(step_z, step_y).start()
    sent = []
    for step_zs in ((0, 1), (2, 3)):

        @pl.loop(0, SIDE)
        def _(trip):
            step_z, pair = step_zs[0] + trip // 2, trip % 2 * 2
            for step_y in (pair, pair + 1):
                right_copy(step_z, step_y).wait()
            for step_y in (pair, pair + 1):
                owner = owner_of(step_z, step_y)
                block = blocks.at[step_z * SIDE + step_y]
                for q in range(4):
                    col = owner * 4 + q
                    lhs = jnp.concatenate(
                        [
                            middle[pairs[(term * 64 + col) * 2 + p], term]
                            for term in range(terms)
                            for p in range(2)
                        ],
                        axis=1,
                    )
                    rhs = jnp.concatenate(
                        [block[term, q, p] for term in range(terms) for p in range(2)], axis=0
                    )
                    product = jnp.dot(lhs, rhs, preferred_element_type=F32)
                    keep = row_live & (lane < size[col])
                    value = jnp.where(keep, product, 0.0).astype(BF16)
                    if q < 2:
                        sum_a[step_z, step_y, :, q * TILE : (q + 1) * TILE] = value
                    else:
                        sum_b[step_y, step_z, :, (q - 2) * TILE : (q - 1) * TILE] = value

        for step_z in step_zs:
            sent.append(
                pltpu.make_async_copy(sum_a.at[step_z], outs_a[step_z], out_sems.at[len(sent)])
            )
            sent[-1].start()
            for k in range(SIDE):
                sent.append(
                    pltpu.make_async_copy(
                        sum_b.at[k, step_z], outs_b[k].at[step_z], out_sems.at[len(sent)]
                    )
                )
                sent[-1].start()
    for copy in sent:
        copy.wait()


def right_stage(arrived, half, right_blocks, place, pairs, size):
    layout = tuple((count, len(blocks) > 1) for count, blocks in zip(CHUNKS, arrived))
    arrived = [block for blocks in arrived for block in blocks]
    terms, rows = right_blocks.shape[0], TILE
    shape = jax.ShapeDtypeStruct((SIDE, rows, 2 * TILE), BF16)
    anywhere = pl.BlockSpec(memory_space=pl.ANY)
    return pl.pallas_call(
        functools.partial(right_kernel, layout, half),
        out_shape=[shape] * 8,
        grid_spec=pltpu.PrefetchScalarGridSpec(
            num_scalar_prefetch=3,
            grid=(1,),
            in_specs=[anywhere] * (len(arrived) + 1),
            out_specs=[anywhere] * 8,
            scratch_shapes=[
                pltpu.VMEM((64, terms, rows, TILE), BF16),
                pltpu.VMEM((GROUP, terms, 4, 2, TILE, TILE), BF16),
                pltpu.VMEM((SIDE, SIDE, rows, 2 * TILE), BF16),
                pltpu.VMEM((SIDE, SIDE, rows, 2 * TILE), BF16),
                pltpu.SemaphoreType.DMA((8 * len(layout),)),
                pltpu.SemaphoreType.DMA((GROUP,)),
                pltpu.SemaphoreType.DMA((SIDE * (SIDE + 1),)),
            ],
        ),
        compiler_params=pltpu.CompilerParams(vmem_limit_bytes=58 << 20),
        cost_estimate=pl.CostEstimate(
            flops=2 * terms * rows * 256 * 8192,
            bytes_accessed=(14 << 20),
            transcendentals=0,
        ),
    )(place, pairs, size, *arrived, right_blocks)


def sum_kernel(*refs):
    inputs, outputs = refs[:8], refs[8:]
    for half in range(2):
        mine = inputs[half * 4 : half * 4 + 4]
        total = mine[0][...].astype(F32)
        for other in mine[1:]:
            total = total + other[...].astype(F32)
        kept = outputs[half * 4 : half * 4 + 4]
        kept[0][...] = total[0]
        for k in range(1, SIDE):
            kept[k][...] = total[k].astype(BF16)


def sum_stage(pieces):
    rows, width = pieces[0].shape[1:]
    whole = pl.BlockSpec(memory_space=pltpu.VMEM)
    kinds = [F32, BF16, BF16, BF16]
    return pl.pallas_call(
        sum_kernel,
        name="near_sum",
        out_shape=[jax.ShapeDtypeStruct((rows, width), kind) for kind in kinds * 2],
        in_specs=[whole] * 8,
        out_specs=[whole] * 8,
        compiler_params=pltpu.CompilerParams(vmem_limit_bytes=16 << 20),
    )(*pieces)


def last_kernel(*refs):
    out = refs[-1]
    rows, width = refs[0].shape
    for block in range(len(refs) // SIDE):
        mine = refs[block * 4 : block * 4 + 4]
        total = mine[0][...]
        for other in mine[1:]:
            total = total + other[...].astype(F32)
        line, col = block // 2 * rows, block % 2 * width
        out[line : line + rows, col : col + width] = total


def last_stage(pieces):
    rows, width = pieces[0].shape
    whole = pl.BlockSpec(memory_space=pltpu.VMEM)
    return pl.pallas_call(
        last_kernel,
        name="far_sum",
        out_shape=jax.ShapeDtypeStruct((rows * len(pieces) // 8, 2 * width), F32),
        in_specs=[whole] * len(pieces),
        out_specs=whole,
        compiler_params=pltpu.CompilerParams(vmem_limit_bytes=16 << 20),
    )(*pieces)


def turn(value, d, along_y):
    return move(value, d, 0) if along_y else move(value, 0, d)


def apply_slab(wave_slab, left_blocks, right_blocks, sector_size, left_pairs, right_pairs):
    group = lax.axis_index("op")
    place = jnp.stack([group // SIDE, group % SIDE, lax.axis_index("bond")]).astype(jnp.int32)
    lefts, rights = left_pairs.reshape(-1), right_pairs.reshape(-1)
    chunk_count = len(CHUNKS)
    starts = [sum(CHUNKS[:chunk]) for chunk in range(chunk_count + 1)]
    wave = wave_slab.reshape(4, TILE, wave_slab.shape[1])
    ahead = min(2, chunk_count)

    def sent_both(values, y_first):
        return [
            [value] + [turn(value, d, (side == 0) == y_first) for d in range(1, SIDE)]
            for side, value in enumerate(values)
        ]

    units = range(starts[ahead])
    values = pack_stage(wave, [], [[(None, side, unit) for unit in units] for side in range(2)])
    got = sent_both(values, False)
    first = sent_both(values, True)
    near = {chunk: ([got[0][1:], got[1][1:]], starts[chunk]) for chunk in range(ahead)}
    arrived = []
    for chunk in range(chunk_count):
        count = CHUNKS[chunk]
        after = chunk + ahead
        sources, offset = near[chunk]
        early = chunk < ahead
        packs = []
        for side in range(2):
            pack = []
            if not early:
                pack += [(None, side, starts[chunk] + unit) for unit in range(count)]
            for d in range(SIDE - 1):
                pack += [(side * 3 + d, side, offset + unit) for unit in range(count)]
            if after < chunk_count:
                pack += [(None, 1 - side, starts[after] + unit) for unit in range(CHUNKS[after])]
            packs.append(pack)
        values = pack_stage(wave, sources[0] + sources[1], packs)
        got = sent_both(values, True)
        pieces, plan = [], []
        for side in range(2):
            for far in range(SIDE):
                slots = range(1, SIDE) if early else range(SIDE)
                plan += [
                    (len(pieces), place_of * count, side, far, slot)
                    for place_of, slot in enumerate(slots)
                ]
                pieces.append(got[side][far])
                if early:
                    plan.append((len(pieces), starts[chunk], side, far, 0))
                    pieces.append(first[side][far])
        if after < chunk_count:
            skip = (SIDE - 1 if early else SIDE) * count
            near[after] = ([got[1][1:], got[0][1:]], skip)
        middles = left_stage(
            pieces,
            tuple(plan),
            MODES[chunk],
            count,
            left_blocks,
            place,
            lefts,
            sector_size,
            starts[chunk],
        )
        for middle in middles:
            arrived.append(exchange(middle))
    finals = []
    for half in range(2):
        mine = arrived[: chunk_count - 1] + [arrived[chunk_count - 1 + half]]
        parts = right_stage(mine, half, right_blocks, place, rights, sector_size)
        got = [parts[0]] + [move(parts[d], 0, d) for d in range(1, SIDE)]
        got += [parts[4]] + [move(parts[4 + d], d, 0) for d in range(1, SIDE)]
        sums = sum_stage(got)
        finals += [sums[0]] + [move(sums[d], d, 0) for d in range(1, SIDE)]
        finals += [sums[4]] + [move(sums[4 + d], 0, d) for d in range(1, SIDE)]
    return last_stage(finals)


def solution(mesh):
    placed = (
        P("op", "bond"),
        P("op", None, None, None, None),
        P("op", None, None, None, None),
        P(),
        P("op", None, None),
        P("op", None, None),
    )
    return jax.shard_map(
        apply_slab, mesh=mesh, in_specs=placed, out_specs=P("bond", "op"), check_vma=False
    )
```

```python
import functools

import jax
import jax.numpy as jnp
from jax import lax
from jax.experimental import pallas as pl
from jax.experimental.pallas import tpu as pltpu
from jax.sharding import PartitionSpec as P


TILE = 128
SIDE = 4
GROUP = SIDE * SIDE
BF16 = jnp.bfloat16
F32 = jnp.float32
CHUNKS = (2, 2, 2, 2)
TURNED = (False, True, False, True)


def move(value, step_y, step_z):
    pairs = [
        (y * SIDE + z, (y + step_y) % SIDE * SIDE + (z + step_z) % SIDE)
        for y in range(SIDE)
        for z in range(SIDE)
    ]
    return lax.ppermute(value, "op", pairs)


def pack_kernel(plans, wave, *refs):
    outs, sems = refs[-len(plans) - 1 : -1], refs[-1]
    gots = refs[: -len(plans) - 1]
    copies = []
    for out, plan in zip(outs, plans):
        for slot, (source, side, unit) in enumerate(plan):
            if source is None:
                block = wave.at[2 * side : 2 * side + 2, :, unit * TILE : (unit + 1) * TILE]
            else:
                block = gots[source].at[unit]
            copies.append(pltpu.make_async_copy(block, out.at[slot], sems.at[len(copies)]))
    for copy in copies:
        copy.start()
    for copy in copies:
        copy.wait()


def pack_stage(wave, gots, plans):
    shapes = [(len(plan), 2, TILE, TILE) for plan in plans]
    return pl.pallas_call(
        functools.partial(pack_kernel, plans),
        out_shape=[jax.ShapeDtypeStruct(shape, BF16) for shape in shapes],
        grid_spec=pltpu.PrefetchScalarGridSpec(
            num_scalar_prefetch=0,
            grid=(1,),
            in_specs=[pl.BlockSpec(memory_space=pl.ANY)] * (1 + len(gots)),
            out_specs=[pl.BlockSpec(shape, lambda i: (0, 0, 0, 0)) for shape in shapes],
            scratch_shapes=[pltpu.SemaphoreType.DMA((sum(len(plan) for plan in plans),))],
        ),
        compiler_params=pltpu.CompilerParams(vmem_limit_bytes=60 << 20),
        cost_estimate=pl.CostEstimate(flops=0, bytes_accessed=3 << 20, transcendentals=0),
    )(wave, *gots)


def left_kernel(first_sector, turned, plan, place, pairs, size, *refs):
    total = 1 + max(entry[0] for entry in plan)
    pieces, left_hbm = refs[:total], refs[total]
    outs = refs[total + 1 : -6]
    whole, left, done, sems, left_sem, out_sems = refs[-6:]
    y, z, bond = place[0], place[1], place[2]
    count = whole.shape[0]

    def left_copy(trip):
        part = pl.ds(trip * 4, 4)
        return pltpu.make_async_copy(left_hbm.at[:, part], left.at[:, part], left_sem.at[trip])

    copies = []
    for source, offset, side, far, near in plan:
        step_y, step_z = (far, near) if side == 0 else (near, far)
        owner = (y + SIDE - step_y) % SIDE * SIDE + (z + SIDE - step_z) % SIDE
        copies.append(
            pltpu.make_async_copy(
                pieces[source].at[offset : offset + count],
                whole.at[:, pl.ds(owner * 4 + 2 * side, 2)],
                sems.at[len(copies)],
            )
        )
    for copy in copies:
        copy.start()
    for trip in range(4):
        left_copy(trip).start()
    lane = lax.broadcasted_iota(jnp.int32, (TILE, TILE), 1)
    strip_sectors = 8
    col_live = jnp.concatenate(
        [
            (lane[:1] < size[bond * strip_sectors + first_sector + s]).astype(F32)
            for s in range(count)
        ],
        axis=1,
    )
    terms, rows = left.shape[0], left.shape[1]
    zero = jnp.zeros((TILE, TILE), BF16)

    def out_copy(block):
        return pltpu.make_async_copy(done.at[block], outs[0].at[block], out_sems.at[block])

    for copy in copies:
        copy.wait()

    @pl.loop(0, rows // 4)
    def _(trip):
        left_copy(trip).wait()
        for u in range(4 * terms):
            row, term = trip * 4 + u // terms, u % terms
            entry = (term * rows + row) * 2
            low, high = pairs[entry], pairs[entry + 1]
            lhs = jnp.concatenate(
                [
                    jnp.where(lane < size[low], left[term, row, 0], zero),
                    jnp.where(lane < size[high], left[term, row, 1], zero),
                ],
                axis=1,
            )
            rhs = jnp.concatenate(
                [
                    jnp.concatenate([whole[s, sector] for s in range(count)], axis=1)
                    for sector in (low, high)
                ],
                axis=0,
            )
            middle = (jnp.dot(lhs, rhs, preferred_element_type=F32) * col_live).astype(BF16)
            target = row // 2
            if turned:
                target = (target // 2 + SIDE - bond // 2) % SIDE * 2 + (target + bond) % 2
            line = u // terms % 2 * TILE
            for s in range(count):
                done[target, s, term, line : line + TILE, :] = middle[
                    :, s * TILE : (s + 1) * TILE
                ]
        if not turned:
            out_copy(trip * 2).start()
            out_copy(trip * 2 + 1).start()

    if turned:
        sent = [
            pltpu.make_async_copy(done.at[block], outs[block], out_sems.at[block])
            for block in range(8)
        ]
        for copy in sent:
            copy.start()
    else:
        sent = [out_copy(block) for block in range(8)]
    for copy in sent:
        copy.wait()


def left_stage(pieces, plan, turned, count, left_blocks, place, pairs, size, first_sector):
    terms = left_blocks.shape[0]
    block = (count, terms, 2 * TILE, TILE)
    shapes = [block] * 8 if turned else [(8, *block)]
    anywhere = pl.BlockSpec(memory_space=pl.ANY)
    return pl.pallas_call(
        functools.partial(left_kernel, first_sector, turned, plan),
        out_shape=[jax.ShapeDtypeStruct(shape, BF16) for shape in shapes],
        grid_spec=pltpu.PrefetchScalarGridSpec(
            num_scalar_prefetch=3,
            grid=(1,),
            in_specs=[anywhere] * (len(pieces) + 1),
            out_specs=[anywhere] * len(shapes),
            scratch_shapes=[
                pltpu.VMEM((count, 64, TILE, TILE), BF16),
                pltpu.VMEM(left_blocks.shape, BF16),
                pltpu.VMEM((8, *block), BF16),
                pltpu.SemaphoreType.DMA((32,)),
                pltpu.SemaphoreType.DMA((4,)),
                pltpu.SemaphoreType.DMA((8,)),
            ],
        ),
        compiler_params=pltpu.CompilerParams(vmem_limit_bytes=60 << 20),
        cost_estimate=pl.CostEstimate(
            flops=2 * terms * 2048 * 256 * count * TILE,
            bytes_accessed=(2 << 20) + (terms * 2048 + 8192) * count * TILE * 2,
            transcendentals=0,
        ),
    )(place, pairs, size, *pieces, left_blocks)


def exchange(blocks):
    if len(blocks) == 1:
        return [lax.all_to_all(blocks[0], "bond", split_axis=0, concat_axis=0, tiled=True)]
    got = [blocks[0]]
    for turned in range(1, 8):
        step_x, step_core = turned // 2, turned % 2
        pairs = [
            (x * 2 + core, (x + step_x) % SIDE * 2 + (core + step_core) % 2)
            for x in range(SIDE)
            for core in range(2)
        ]
        got.append(lax.ppermute(blocks[turned], "bond", pairs))
    return got


def right_kernel(layout, place, pairs, size, *refs):
    total = sum(8 if turned else 1 for _, turned in layout)
    arrived, right = list(refs[:total]), refs[total]
    outs_a, outs_b = refs[total + 1 : total + 5], refs[total + 5 : total + 9]
    middle, blocks, sum_a, sum_b, sems, right_sems, out_sems = refs[total + 9 :]
    bond = place[2]
    rows, terms = middle.shape[2], middle.shape[1]
    copies = []
    first = 0
    for count, turned in layout:
        whole = None if turned else arrived.pop(0)
        for block in range(8):
            source = block
            piece = arrived.pop(0) if turned else whole.at[block]
            if turned:
                source = (bond // 2 + SIDE - block // 2) % SIDE * 2 + (bond + block) % 2
            copies.append(
                pltpu.make_async_copy(
                    piece, middle.at[pl.ds(source * 8 + first, count)], sems.at[len(copies)]
                )
            )
        first += count
    for copy in copies:
        copy.start()

    def owner_of(step_z, step_y):
        return (place[0] + step_y) % SIDE * SIDE + (place[1] + step_z) % SIDE

    def right_copy(step_z, step_y):
        return pltpu.make_async_copy(
            right.at[:, pl.ds(owner_of(step_z, step_y) * 4, 4)],
            blocks.at[step_z * SIDE + step_y],
            right_sems.at[step_z * SIDE + step_y],
        )

    for step_y in range(SIDE):
        right_copy(0, step_y).start()
    line = lax.broadcasted_iota(jnp.int32, (TILE, TILE), 0)
    lane = lax.broadcasted_iota(jnp.int32, (TILE, TILE), 1)
    row_live = jnp.concatenate([line < size[bond * 2 + h] for h in range(rows // TILE)], axis=0)
    lanes = jnp.concatenate([lane] * (rows // TILE), axis=0)
    for copy in copies:
        copy.wait()
    for step_z in range(1, SIDE):
        for step_y in range(SIDE):
            right_copy(step_z, step_y).start()
    sent = []
    for step_zs in ((0, 1), (2, 3)):

        @pl.loop(0, SIDE)
        def _(trip):
            step_z, pair = step_zs[0] + trip // 2, trip % 2 * 2
            for step_y in (pair, pair + 1):
                right_copy(step_z, step_y).wait()
            for step_y in (pair, pair + 1):
                owner = owner_of(step_z, step_y)
                block = blocks.at[step_z * SIDE + step_y]
                for q in range(4):
                    col = owner * 4 + q
                    lhs = jnp.concatenate(
                        [
                            middle[pairs[(term * 64 + col) * 2 + p], term]
                            for term in range(terms)
                            for p in range(2)
                        ],
                        axis=1,
                    )
                    rhs = jnp.concatenate(
                        [block[term, q, p] for term in range(terms) for p in range(2)], axis=0
                    )
                    product = jnp.dot(lhs, rhs, preferred_element_type=F32)
                    keep = row_live & (lanes < size[col])
                    value = jnp.where(keep, product, 0.0).astype(BF16)
                    if q < 2:
                        sum_a[step_z, step_y, :, q * TILE : (q + 1) * TILE] = value
                    else:
                        sum_b[step_y, step_z, :, (q - 2) * TILE : (q - 1) * TILE] = value

        for step_z in step_zs:
            sent.append(
                pltpu.make_async_copy(sum_a.at[step_z], outs_a[step_z], out_sems.at[len(sent)])
            )
            sent[-1].start()
            for k in range(SIDE):
                sent.append(
                    pltpu.make_async_copy(
                        sum_b.at[k, step_z], outs_b[k].at[step_z], out_sems.at[len(sent)]
                    )
                )
                sent[-1].start()
    for copy in sent:
        copy.wait()


def right_stage(arrived, right_blocks, place, pairs, size):
    layout = tuple((count, len(blocks) > 1) for count, blocks in zip(CHUNKS, arrived))
    arrived = [block for blocks in arrived for block in blocks]
    terms, rows = right_blocks.shape[0], 2 * TILE
    shape = jax.ShapeDtypeStruct((SIDE, rows, 2 * TILE), BF16)
    anywhere = pl.BlockSpec(memory_space=pl.ANY)
    return pl.pallas_call(
        functools.partial(right_kernel, layout),
        name="right",
        out_shape=[shape] * 8,
        grid_spec=pltpu.PrefetchScalarGridSpec(
            num_scalar_prefetch=3,
            grid=(1,),
            in_specs=[anywhere] * (len(arrived) + 1),
            out_specs=[anywhere] * 8,
            scratch_shapes=[
                pltpu.VMEM((64, terms, rows, TILE), BF16),
                pltpu.VMEM((GROUP, terms, 4, 2, TILE, TILE), BF16),
                pltpu.VMEM((SIDE, SIDE, rows, 2 * TILE), BF16),
                pltpu.VMEM((SIDE, SIDE, rows, 2 * TILE), BF16),
                pltpu.SemaphoreType.DMA((8 * len(layout),)),
                pltpu.SemaphoreType.DMA((GROUP,)),
                pltpu.SemaphoreType.DMA((SIDE * (SIDE + 1),)),
            ],
        ),
        compiler_params=pltpu.CompilerParams(vmem_limit_bytes=60 << 20),
        cost_estimate=pl.CostEstimate(
            flops=2 * terms * rows * 256 * 8192,
            bytes_accessed=(20 << 20),
            transcendentals=0,
        ),
    )(place, pairs, size, *arrived, right_blocks)


def sum_kernel(*refs):
    inputs, outputs = refs[:8], refs[8:]
    for half in range(2):
        mine = inputs[half * 4 : half * 4 + 4]
        total = mine[0][...].astype(F32)
        for other in mine[1:]:
            total = total + other[...].astype(F32)
        kept = outputs[half * 4 : half * 4 + 4]
        kept[0][...] = total[0]
        for k in range(1, SIDE):
            kept[k][...] = total[k].astype(BF16)


def sum_stage(pieces):
    rows, width = pieces[0].shape[1:]
    whole = pl.BlockSpec(memory_space=pltpu.VMEM)
    kinds = [F32, BF16, BF16, BF16]
    return pl.pallas_call(
        sum_kernel,
        name="near_sum",
        out_shape=[jax.ShapeDtypeStruct((rows, width), kind) for kind in kinds * 2],
        in_specs=[whole] * 8,
        out_specs=[whole] * 8,
        compiler_params=pltpu.CompilerParams(vmem_limit_bytes=16 << 20),
    )(*pieces)


def last_kernel(*refs):
    out = refs[-1]
    rows, width = refs[0].shape
    for block in range(len(refs) // SIDE):
        mine = refs[block * 4 : block * 4 + 4]
        total = mine[0][...]
        for other in mine[1:]:
            total = total + other[...].astype(F32)
        line, col = block // 2 * rows, block % 2 * width
        out[line : line + rows, col : col + width] = total


def last_stage(pieces):
    rows, width = pieces[0].shape
    whole = pl.BlockSpec(memory_space=pltpu.VMEM)
    return pl.pallas_call(
        last_kernel,
        name="far_sum",
        out_shape=jax.ShapeDtypeStruct((rows * len(pieces) // 8, 2 * width), F32),
        in_specs=[whole] * len(pieces),
        out_specs=whole,
        compiler_params=pltpu.CompilerParams(vmem_limit_bytes=16 << 20),
    )(*pieces)


def turn(value, d, along_y):
    return move(value, d, 0) if along_y else move(value, 0, d)


def apply_slab(wave_slab, left_blocks, right_blocks, sector_size, left_pairs, right_pairs):
    group = lax.axis_index("op")
    place = jnp.stack([group // SIDE, group % SIDE, lax.axis_index("bond")]).astype(jnp.int32)
    lefts, rights = left_pairs.reshape(-1), right_pairs.reshape(-1)
    chunk_count = len(CHUNKS)
    starts = [sum(CHUNKS[:chunk]) for chunk in range(chunk_count + 1)]
    wave = wave_slab.reshape(4, TILE, wave_slab.shape[1])
    ahead = min(2, chunk_count)

    def sent_both(values, y_first):
        return [
            [value] + [turn(value, d, (side == 0) == y_first) for d in range(1, SIDE)]
            for side, value in enumerate(values)
        ]

    units = range(starts[ahead])
    values = pack_stage(wave, [], [[(None, side, unit) for unit in units] for side in range(2)])
    got = sent_both(values, False)
    first = sent_both(values, True)
    near = {chunk: ([got[0][1:], got[1][1:]], starts[chunk]) for chunk in range(ahead)}
    arrived = []
    for chunk in range(chunk_count):
        count = CHUNKS[chunk]
        after = chunk + ahead
        sources, offset = near[chunk]
        early = chunk < ahead
        packs = []
        for side in range(2):
            pack = []
            if not early:
                pack += [(None, side, starts[chunk] + unit) for unit in range(count)]
            for d in range(SIDE - 1):
                pack += [(side * 3 + d, side, offset + unit) for unit in range(count)]
            if after < chunk_count:
                pack += [(None, 1 - side, starts[after] + unit) for unit in range(CHUNKS[after])]
            packs.append(pack)
        values = pack_stage(wave, sources[0] + sources[1], packs)
        got = sent_both(values, True)
        pieces, plan = [], []
        for side in range(2):
            for far in range(SIDE):
                slots = range(1, SIDE) if early else range(SIDE)
                plan += [
                    (len(pieces), place_of * count, side, far, slot)
                    for place_of, slot in enumerate(slots)
                ]
                pieces.append(got[side][far])
                if early:
                    plan.append((len(pieces), starts[chunk], side, far, 0))
                    pieces.append(first[side][far])
        if after < chunk_count:
            skip = (SIDE - 1 if early else SIDE) * count
            near[after] = ([got[1][1:], got[0][1:]], skip)
        middles = left_stage(
            pieces,
            tuple(plan),
            TURNED[chunk],
            count,
            left_blocks,
            place,
            lefts,
            sector_size,
            starts[chunk],
        )
        arrived.append(exchange(middles))
    parts = right_stage(arrived, right_blocks, place, rights, sector_size)
    got = [parts[0]] + [move(parts[d], 0, d) for d in range(1, SIDE)]
    got += [parts[4]] + [move(parts[4 + d], d, 0) for d in range(1, SIDE)]
    sums = sum_stage(got)
    finals = [sums[0]] + [move(sums[d], d, 0) for d in range(1, SIDE)]
    finals += [sums[4]] + [move(sums[4 + d], 0, d) for d in range(1, SIDE)]
    return last_stage(finals)


def solution(mesh):
    placed = (
        P("op", "bond"),
        P("op", None, None, None, None),
        P("op", None, None, None, None),
        P(),
        P("op", None, None),
        P("op", None, None),
    )
    return jax.shard_map(
        apply_slab, mesh=mesh, in_specs=placed, out_specs=P("bond", "op"), check_vma=False
    )
```

```python
import functools

import jax
import jax.numpy as jnp
from jax import lax
from jax.experimental import pallas as pl
from jax.experimental.pallas import tpu as pltpu
from jax.sharding import PartitionSpec as P


TILE = 128
SIDE = 4
GROUP = SIDE * SIDE
BF16 = jnp.bfloat16
F32 = jnp.float32
CHUNKS = (2, 2, 2, 2)
SPLIT = (192, 64)
MODES = (
    ((False, 0, 256),),
    ((True, 0, 256),),
    ((False, 0, 256),),
    ((True, 0, SPLIT[0]), (False, SPLIT[0], SPLIT[1])),
)


def move(value, step_y, step_z):
    pairs = [
        (y * SIDE + z, (y + step_y) % SIDE * SIDE + (z + step_z) % SIDE)
        for y in range(SIDE)
        for z in range(SIDE)
    ]
    return lax.ppermute(value, "op", pairs)


def pack_kernel(plans, wave, *refs):
    outs, sems = refs[-len(plans) - 1 : -1], refs[-1]
    gots = refs[: -len(plans) - 1]
    copies = []
    for out, plan in zip(outs, plans):
        for slot, (source, side, unit) in enumerate(plan):
            if source is None:
                block = wave.at[2 * side : 2 * side + 2, :, unit * TILE : (unit + 1) * TILE]
            else:
                block = gots[source].at[unit]
            copies.append(pltpu.make_async_copy(block, out.at[slot], sems.at[len(copies)]))
    for copy in copies:
        copy.start()
    for copy in copies:
        copy.wait()


def pack_stage(wave, gots, plans):
    shapes = [(len(plan), 2, TILE, TILE) for plan in plans]
    return pl.pallas_call(
        functools.partial(pack_kernel, plans),
        out_shape=[jax.ShapeDtypeStruct(shape, BF16) for shape in shapes],
        grid_spec=pltpu.PrefetchScalarGridSpec(
            num_scalar_prefetch=0,
            grid=(1,),
            in_specs=[pl.BlockSpec(memory_space=pl.ANY)] * (1 + len(gots)),
            out_specs=[pl.BlockSpec(shape, lambda i: (0, 0, 0, 0)) for shape in shapes],
            scratch_shapes=[pltpu.SemaphoreType.DMA((sum(len(plan) for plan in plans),))],
        ),
        compiler_params=pltpu.CompilerParams(vmem_limit_bytes=8 << 20),
        cost_estimate=pl.CostEstimate(flops=0, bytes_accessed=3 << 20, transcendentals=0),
    )(wave, *gots)


def left_kernel(first_sector, modes, plan, place, pairs, size, *refs):
    total = 1 + max(entry[0] for entry in plan)
    pieces, left_hbm = refs[:total], refs[total]
    rest = refs[total + 1 :]
    out_count = sum(8 if turned else 1 for turned, _, _ in modes)
    outs, rest = list(rest[:out_count]), rest[out_count:]
    whole, left, sems, left_sem, out_sems = rest[:5]
    dones = rest[5:]
    targets = []
    for turned, _, _ in modes:
        targets.append([outs.pop(0) for _ in range(8 if turned else 1)])
    y, z, bond = place[0], place[1], place[2]
    count = whole.shape[0]

    def left_copy(trip):
        part = pl.ds(trip * 4, 4)
        return pltpu.make_async_copy(left_hbm.at[:, part], left.at[:, part], left_sem.at[trip])

    copies = []
    for source, offset, side, far, near in plan:
        step_y, step_z = (far, near) if side == 0 else (near, far)
        owner = (y + SIDE - step_y) % SIDE * SIDE + (z + SIDE - step_z) % SIDE
        copies.append(
            pltpu.make_async_copy(
                pieces[source].at[offset : offset + count],
                whole.at[:, pl.ds(owner * 4 + 2 * side, 2)],
                sems.at[len(copies)],
            )
        )
    for copy in copies:
        copy.start()
    for trip in range(4):
        left_copy(trip).start()
    lane = lax.broadcasted_iota(jnp.int32, (TILE, TILE), 1)
    strip_sectors = 8
    col_live = jnp.concatenate(
        [
            (lane[:1] < size[bond * strip_sectors + first_sector + s]).astype(F32)
            for s in range(count)
        ],
        axis=1,
    )
    terms, rows = left.shape[0], left.shape[1]
    zero = jnp.zeros((TILE, TILE), BF16)

    def out_copy(mode, block):
        target = targets[mode]
        ref = target[block] if len(target) == 8 else target[0].at[block]
        return pltpu.make_async_copy(dones[mode].at[block], ref, out_sems.at[mode, block])

    for copy in copies:
        copy.wait()

    @pl.loop(0, rows // 4)
    def _(trip):
        left_copy(trip).wait()
        for u in range(4 * terms):
            row, term = trip * 4 + u // terms, u % terms
            entry = (term * rows + row) * 2
            low, high = pairs[entry], pairs[entry + 1]
            lhs = jnp.concatenate(
                [
                    jnp.where(lane < size[low], left[term, row, 0], zero),
                    jnp.where(lane < size[high], left[term, row, 1], zero),
                ],
                axis=1,
            )
            rhs = jnp.concatenate(
                [
                    jnp.concatenate([whole[s, sector] for s in range(count)], axis=1)
                    for sector in (low, high)
                ],
                axis=0,
            )
            middle = (jnp.dot(lhs, rhs, preferred_element_type=F32) * col_live).astype(BF16)
            for mode, (turned, start, length) in enumerate(modes):
                low_row = max(start, u // terms % 2 * TILE)
                high_row = min(start + length, u // terms % 2 * TILE + TILE)
                if low_row >= high_row:
                    continue
                target = row // 2
                if turned:
                    target = (target // 2 + SIDE - bond // 2) % SIDE * 2 + (target + bond) % 2
                shift = u // terms % 2 * TILE
                for s in range(count):
                    dones[mode][target, s, term, low_row - start : high_row - start, :] = middle[
                        low_row - shift : high_row - shift, s * TILE : (s + 1) * TILE
                    ]
        for mode, (turned, _, _) in enumerate(modes):
            if not turned:
                out_copy(mode, trip * 2).start()
                out_copy(mode, trip * 2 + 1).start()

    for mode, (turned, _, _) in enumerate(modes):
        if turned:
            for block in range(8):
                out_copy(mode, block).start()
    for mode in range(len(modes)):
        for block in range(8):
            out_copy(mode, block).wait()


def left_stage(pieces, plan, modes, count, left_blocks, place, pairs, size, first_sector):
    terms = left_blocks.shape[0]
    blocks = [(count, terms, length, TILE) for _, _, length in modes]
    shapes = []
    for (turned, _, _), block in zip(modes, blocks):
        shapes += [block] * 8 if turned else [(8, *block)]
    anywhere = pl.BlockSpec(memory_space=pl.ANY)
    results = pl.pallas_call(
        functools.partial(left_kernel, first_sector, modes, plan),
        out_shape=[jax.ShapeDtypeStruct(shape, BF16) for shape in shapes],
        grid_spec=pltpu.PrefetchScalarGridSpec(
            num_scalar_prefetch=3,
            grid=(1,),
            in_specs=[anywhere] * (len(pieces) + 1),
            out_specs=[anywhere] * len(shapes),
            scratch_shapes=[
                pltpu.VMEM((count, 64, TILE, TILE), BF16),
                pltpu.VMEM(left_blocks.shape, BF16),
                pltpu.SemaphoreType.DMA((32,)),
                pltpu.SemaphoreType.DMA((4,)),
                pltpu.SemaphoreType.DMA((len(modes), 8)),
            ]
            + [pltpu.VMEM((8, *block), BF16) for block in blocks],
        ),
        compiler_params=pltpu.CompilerParams(vmem_limit_bytes=60 << 20),
        cost_estimate=pl.CostEstimate(
            flops=2 * terms * 2048 * 256 * count * TILE,
            bytes_accessed=(2 << 20) + (terms * 2048 + 8192) * count * TILE * 2,
            transcendentals=0,
        ),
    )(place, pairs, size, *pieces, left_blocks)
    results = list(results)
    return [[results.pop(0) for _ in range(8 if turned else 1)] for turned, _, _ in modes]


def exchange(blocks):
    if len(blocks) == 1:
        return [lax.all_to_all(blocks[0], "bond", split_axis=0, concat_axis=0, tiled=True)]
    got = [blocks[0]]
    for turned in range(1, 8):
        step_x, step_core = turned // 2, turned % 2
        pairs = [
            (x * 2 + core, (x + step_x) % SIDE * 2 + (core + step_core) % 2)
            for x in range(SIDE)
            for core in range(2)
        ]
        got.append(lax.ppermute(blocks[turned], "bond", pairs))
    return got


def right_kernel(layout, half, place, pairs, size, *refs):
    total = sum(8 if turned else 1 for _, turned in layout)
    arrived, right = list(refs[:total]), refs[total]
    rest = refs[total + 1 :]
    if half == 0:
        outs_a, outs_b, rest = rest[:4], rest[4:8], rest[8:]
    else:
        out, rest = rest[0], rest[1:]
    middle, blocks, sum_a, sum_b, sems, right_sems, out_sems = rest
    first_row = sum(SPLIT[:half])
    bond = place[2]
    rows, terms = middle.shape[2], middle.shape[1]
    copies = []
    first = 0
    for count, turned in layout:
        whole = None if turned else arrived.pop(0)
        for block in range(8):
            source = block
            piece = arrived.pop(0) if turned else whole.at[block]
            if turned:
                source = (bond // 2 + SIDE - block // 2) % SIDE * 2 + (bond + block) % 2
            if piece.shape[2] != rows:
                piece = piece.at[:, :, first_row : first_row + rows]
            copies.append(
                pltpu.make_async_copy(
                    piece, middle.at[pl.ds(source * 8 + first, count)], sems.at[len(copies)]
                )
            )
        first += count
    for copy in copies:
        copy.start()

    def owner_of(step_z, step_y):
        return (place[0] + step_y) % SIDE * SIDE + (place[1] + step_z) % SIDE

    def right_copy(step_z, step_y):
        return pltpu.make_async_copy(
            right.at[:, pl.ds(owner_of(step_z, step_y) * 4, 4)],
            blocks.at[step_z * SIDE + step_y],
            right_sems.at[step_z * SIDE + step_y],
        )

    for step_y in range(SIDE):
        right_copy(0, step_y).start()
    lane = lax.broadcasted_iota(jnp.int32, (rows, TILE), 1)
    lives = []
    for h in range(2):
        low, high = max(first_row, h * TILE), min(first_row + rows, (h + 1) * TILE)
        if low < high:
            line = lax.broadcasted_iota(jnp.int32, (high - low, TILE), 0) + (low - h * TILE)
            lives.append(line < size[bond * 2 + h])
    row_live = jnp.concatenate(lives, axis=0)
    for copy in copies:
        copy.wait()
    for step_z in range(1, SIDE):
        for step_y in range(SIDE):
            right_copy(step_z, step_y).start()
    sent = []
    for step_zs in ((0, 1), (2, 3)):

        @pl.loop(0, SIDE)
        def _(trip):
            step_z, pair = step_zs[0] + trip // 2, trip % 2 * 2
            for step_y in (pair, pair + 1):
                right_copy(step_z, step_y).wait()
            for step_y in (pair, pair + 1):
                owner = owner_of(step_z, step_y)
                block = blocks.at[step_z * SIDE + step_y]
                for q in range(4):
                    col = owner * 4 + q
                    lhs = jnp.concatenate(
                        [
                            middle[pairs[(term * 64 + col) * 2 + p], term]
                            for term in range(terms)
                            for p in range(2)
                        ],
                        axis=1,
                    )
                    rhs = jnp.concatenate(
                        [block[term, q, p] for term in range(terms) for p in range(2)], axis=0
                    )
                    product = jnp.dot(lhs, rhs, preferred_element_type=F32)
                    keep = row_live & (lane < size[col])
                    value = jnp.where(keep, product, 0.0).astype(BF16)
                    if half == 1:
                        sum_a[owner, :, q * TILE : (q + 1) * TILE] = value
                    elif q < 2:
                        sum_a[step_z, step_y, :, q * TILE : (q + 1) * TILE] = value
                    else:
                        sum_b[step_y, step_z, :, (q - 2) * TILE : (q - 1) * TILE] = value

        for step_z in step_zs if half == 0 else ():
            sent.append(
                pltpu.make_async_copy(sum_a.at[step_z], outs_a[step_z], out_sems.at[len(sent)])
            )
            sent[-1].start()
            for k in range(SIDE):
                sent.append(
                    pltpu.make_async_copy(
                        sum_b.at[k, step_z], outs_b[k].at[step_z], out_sems.at[len(sent)]
                    )
                )
                sent[-1].start()
    if half == 1:
        sent.append(pltpu.make_async_copy(sum_a, out, out_sems.at[0]))
        sent[-1].start()
    for copy in sent:
        copy.wait()


def right_stage(arrived, half, right_blocks, place, pairs, size):
    layout = tuple((count, len(blocks) > 1) for count, blocks in zip(CHUNKS, arrived))
    arrived = [block for blocks in arrived for block in blocks]
    terms, rows = right_blocks.shape[0], SPLIT[half]
    if half == 0:
        shapes = [jax.ShapeDtypeStruct((SIDE, rows, 2 * TILE), BF16)] * 8
        scratch = [pltpu.VMEM((SIDE, SIDE, rows, 2 * TILE), BF16)] * 2
    else:
        shapes = [jax.ShapeDtypeStruct((GROUP, rows, 4 * TILE), BF16)]
        scratch = [pltpu.VMEM(shapes[0].shape, BF16), pltpu.VMEM((16, TILE), BF16)]
    anywhere = pl.BlockSpec(memory_space=pl.ANY)
    return pl.pallas_call(
        functools.partial(right_kernel, layout, half),
        out_shape=shapes,
        grid_spec=pltpu.PrefetchScalarGridSpec(
            num_scalar_prefetch=3,
            grid=(1,),
            in_specs=[anywhere] * (len(arrived) + 1),
            out_specs=[anywhere] * len(shapes),
            scratch_shapes=[
                pltpu.VMEM((64, terms, rows, TILE), BF16),
                pltpu.VMEM((GROUP, terms, 4, 2, TILE, TILE), BF16),
                *scratch,
                pltpu.SemaphoreType.DMA((8 * len(layout),)),
                pltpu.SemaphoreType.DMA((GROUP,)),
                pltpu.SemaphoreType.DMA((SIDE * (SIDE + 1),)),
            ],
        ),
        compiler_params=pltpu.CompilerParams(vmem_limit_bytes=58 << 20),
        cost_estimate=pl.CostEstimate(
            flops=2 * terms * rows * 256 * 8192,
            bytes_accessed=(14 << 20),
            transcendentals=0,
        ),
    )(place, pairs, size, *arrived, right_blocks)


def sum_kernel(*refs):
    inputs, outputs = refs[:8], refs[8:]
    for half in range(2):
        mine = inputs[half * 4 : half * 4 + 4]
        total = mine[0][...].astype(F32)
        for other in mine[1:]:
            total = total + other[...].astype(F32)
        kept = outputs[half * 4 : half * 4 + 4]
        kept[0][...] = total[0]
        for k in range(1, SIDE):
            kept[k][...] = total[k].astype(BF16)


def sum_stage(pieces):
    rows, width = pieces[0].shape[1:]
    whole = pl.BlockSpec(memory_space=pltpu.VMEM)
    kinds = [F32, BF16, BF16, BF16]
    return pl.pallas_call(
        sum_kernel,
        name="near_sum",
        out_shape=[jax.ShapeDtypeStruct((rows, width), kind) for kind in kinds * 2],
        in_specs=[whole] * 8,
        out_specs=[whole] * 8,
        compiler_params=pltpu.CompilerParams(vmem_limit_bytes=16 << 20),
    )(*pieces)


def last_kernel(*refs):
    block, out = refs[-2], refs[-1]
    rows, width = refs[0].shape
    for side in range(2):
        mine = refs[side * 4 : side * 4 + 4]
        total = mine[0][...]
        for other in mine[1:]:
            total = total + other[...].astype(F32)
        out[:rows, side * width : (side + 1) * width] = total
    total = block[0].astype(F32)
    for source in range(1, GROUP):
        total = total + block[source].astype(F32)
    out[rows:, :] = total


def last_stage(pieces):
    rows, width = sum(SPLIT), 4 * TILE
    whole = pl.BlockSpec(memory_space=pltpu.VMEM)
    return pl.pallas_call(
        last_kernel,
        name="far_sum",
        out_shape=jax.ShapeDtypeStruct((rows, width), F32),
        in_specs=[whole] * len(pieces),
        out_specs=whole,
        compiler_params=pltpu.CompilerParams(vmem_limit_bytes=16 << 20),
    )(*pieces)


def turn(value, d, along_y):
    return move(value, d, 0) if along_y else move(value, 0, d)


def apply_slab(wave_slab, left_blocks, right_blocks, sector_size, left_pairs, right_pairs):
    group = lax.axis_index("op")
    place = jnp.stack([group // SIDE, group % SIDE, lax.axis_index("bond")]).astype(jnp.int32)
    lefts, rights = left_pairs.reshape(-1), right_pairs.reshape(-1)
    chunk_count = len(CHUNKS)
    starts = [sum(CHUNKS[:chunk]) for chunk in range(chunk_count + 1)]
    wave = wave_slab.reshape(4, TILE, wave_slab.shape[1])
    ahead = min(2, chunk_count)

    def sent_both(values, y_first):
        return [
            [value] + [turn(value, d, (side == 0) == y_first) for d in range(1, SIDE)]
            for side, value in enumerate(values)
        ]

    units = range(starts[ahead])
    values = pack_stage(wave, [], [[(None, side, unit) for unit in units] for side in range(2)])
    got = sent_both(values, False)
    first = sent_both(values, True)
    near = {chunk: ([got[0][1:], got[1][1:]], starts[chunk]) for chunk in range(ahead)}
    arrived = []
    for chunk in range(chunk_count):
        count = CHUNKS[chunk]
        after = chunk + ahead
        sources, offset = near[chunk]
        early = chunk < ahead
        packs = []
        for side in range(2):
            pack = []
            if not early:
                pack += [(None, side, starts[chunk] + unit) for unit in range(count)]
            for d in range(SIDE - 1):
                pack += [(side * 3 + d, side, offset + unit) for unit in range(count)]
            if after < chunk_count:
                pack += [(None, 1 - side, starts[after] + unit) for unit in range(CHUNKS[after])]
            packs.append(pack)
        values = pack_stage(wave, sources[0] + sources[1], packs)
        got = sent_both(values, True)
        pieces, plan = [], []
        for side in range(2):
            for far in range(SIDE):
                slots = range(1, SIDE) if early else range(SIDE)
                plan += [
                    (len(pieces), place_of * count, side, far, slot)
                    for place_of, slot in enumerate(slots)
                ]
                pieces.append(got[side][far])
                if early:
                    plan.append((len(pieces), starts[chunk], side, far, 0))
                    pieces.append(first[side][far])
        if after < chunk_count:
            skip = (SIDE - 1 if early else SIDE) * count
            near[after] = ([got[1][1:], got[0][1:]], skip)
        middles = left_stage(
            pieces,
            tuple(plan),
            MODES[chunk],
            count,
            left_blocks,
            place,
            lefts,
            sector_size,
            starts[chunk],
        )
        for middle in middles:
            arrived.append(exchange(middle))
    parts = []
    for half in range(2):
        mine = arrived[: chunk_count - 1] + [arrived[chunk_count - 1 + half]]
        parts.append(right_stage(mine, half, right_blocks, place, rights, sector_size))
    block = lax.all_to_all(parts[1][0], "op", split_axis=0, concat_axis=0, tiled=True)
    parts = parts[0]
    got = [parts[0]] + [move(parts[d], 0, d) for d in range(1, SIDE)]
    got += [parts[4]] + [move(parts[4 + d], d, 0) for d in range(1, SIDE)]
    sums = sum_stage(got)
    finals = [sums[0]] + [move(sums[d], d, 0) for d in range(1, SIDE)]
    finals += [sums[4]] + [move(sums[4 + d], 0, d) for d in range(1, SIDE)]
    finals.append(block)
    return last_stage(finals)


def solution(mesh):
    placed = (
        P("op", "bond"),
        P("op", None, None, None, None),
        P("op", None, None, None, None),
        P(),
        P("op", None, None),
        P("op", None, None),
    )
    return jax.shard_map(
        apply_slab, mesh=mesh, in_specs=placed, out_specs=P("bond", "op"), check_vma=False
    )
```

```python
import functools

import jax
import jax.numpy as jnp
from jax import lax
from jax.experimental import pallas as pl
from jax.experimental.pallas import tpu as pltpu
from jax.sharding import PartitionSpec as P


TILE = 128
SIDE = 4
GROUP = SIDE * SIDE
BF16 = jnp.bfloat16
F32 = jnp.float32
CHUNKS = (2, 2, 2, 2)
SPLIT = (160, 96)
MODES = (
    ((False, 0, 256),),
    ((True, 0, 256),),
    ((False, 0, 256),),
    ((True, 0, SPLIT[0]), (False, SPLIT[0], SPLIT[1])),
)


def move(value, step_y, step_z):
    pairs = [
        (y * SIDE + z, (y + step_y) % SIDE * SIDE + (z + step_z) % SIDE)
        for y in range(SIDE)
        for z in range(SIDE)
    ]
    return lax.ppermute(value, "op", pairs)


def pack_kernel(plans, wave, *refs):
    outs, sems = refs[-len(plans) - 1 : -1], refs[-1]
    gots = refs[: -len(plans) - 1]
    copies = []
    for out, plan in zip(outs, plans):
        for slot, (source, side, unit) in enumerate(plan):
            if source is None:
                block = wave.at[2 * side : 2 * side + 2, :, unit * TILE : (unit + 1) * TILE]
            else:
                block = gots[source].at[unit]
            copies.append(pltpu.make_async_copy(block, out.at[slot], sems.at[len(copies)]))
    for copy in copies:
        copy.start()
    for copy in copies:
        copy.wait()


def pack_stage(wave, gots, plans):
    shapes = [(len(plan), 2, TILE, TILE) for plan in plans]
    return pl.pallas_call(
        functools.partial(pack_kernel, plans),
        out_shape=[jax.ShapeDtypeStruct(shape, BF16) for shape in shapes],
        grid_spec=pltpu.PrefetchScalarGridSpec(
            num_scalar_prefetch=0,
            grid=(1,),
            in_specs=[pl.BlockSpec(memory_space=pl.ANY)] * (1 + len(gots)),
            out_specs=[pl.BlockSpec(shape, lambda i: (0, 0, 0, 0)) for shape in shapes],
            scratch_shapes=[pltpu.SemaphoreType.DMA((sum(len(plan) for plan in plans),))],
        ),
        compiler_params=pltpu.CompilerParams(vmem_limit_bytes=8 << 20),
        cost_estimate=pl.CostEstimate(flops=0, bytes_accessed=3 << 20, transcendentals=0),
    )(wave, *gots)


def left_kernel(first_sector, modes, plan, place, pairs, size, *refs):
    total = 1 + max(entry[0] for entry in plan)
    pieces, left_hbm = refs[:total], refs[total]
    rest = refs[total + 1 :]
    out_count = sum(8 if turned else 1 for turned, _, _ in modes)
    outs, rest = list(rest[:out_count]), rest[out_count:]
    whole, left, sems, left_sem, out_sems = rest[:5]
    dones = rest[5:]
    targets = []
    for turned, _, _ in modes:
        targets.append([outs.pop(0) for _ in range(8 if turned else 1)])
    y, z, bond = place[0], place[1], place[2]
    count = whole.shape[0]

    def left_copy(trip):
        part = pl.ds(trip * 4, 4)
        return pltpu.make_async_copy(left_hbm.at[:, part], left.at[:, part], left_sem.at[trip])

    copies = []
    for source, offset, side, far, near in plan:
        step_y, step_z = (far, near) if side == 0 else (near, far)
        owner = (y + SIDE - step_y) % SIDE * SIDE + (z + SIDE - step_z) % SIDE
        copies.append(
            pltpu.make_async_copy(
                pieces[source].at[offset : offset + count],
                whole.at[:, pl.ds(owner * 4 + 2 * side, 2)],
                sems.at[len(copies)],
            )
        )
    for copy in copies:
        copy.start()
    for trip in range(4):
        left_copy(trip).start()
    lane = lax.broadcasted_iota(jnp.int32, (TILE, TILE), 1)
    strip_sectors = 8
    col_live = jnp.concatenate(
        [
            (lane[:1] < size[bond * strip_sectors + first_sector + s]).astype(F32)
            for s in range(count)
        ],
        axis=1,
    )
    terms, rows = left.shape[0], left.shape[1]
    zero = jnp.zeros((TILE, TILE), BF16)

    def out_copy(mode, block):
        target = targets[mode]
        ref = target[block] if len(target) == 8 else target[0].at[block]
        return pltpu.make_async_copy(dones[mode].at[block], ref, out_sems.at[mode, block])

    for copy in copies:
        copy.wait()

    @pl.loop(0, rows // 4)
    def _(trip):
        left_copy(trip).wait()
        for u in range(4 * terms):
            row, term = trip * 4 + u // terms, u % terms
            entry = (term * rows + row) * 2
            low, high = pairs[entry], pairs[entry + 1]
            lhs = jnp.concatenate(
                [
                    jnp.where(lane < size[low], left[term, row, 0], zero),
                    jnp.where(lane < size[high], left[term, row, 1], zero),
                ],
                axis=1,
            )
            rhs = jnp.concatenate(
                [
                    jnp.concatenate([whole[s, sector] for s in range(count)], axis=1)
                    for sector in (low, high)
                ],
                axis=0,
            )
            middle = (jnp.dot(lhs, rhs, preferred_element_type=F32) * col_live).astype(BF16)
            for mode, (turned, start, length) in enumerate(modes):
                low_row = max(start, u // terms % 2 * TILE)
                high_row = min(start + length, u // terms % 2 * TILE + TILE)
                if low_row >= high_row:
                    continue
                target = row // 2
                if turned:
                    target = (target // 2 + SIDE - bond // 2) % SIDE * 2 + (target + bond) % 2
                shift = u // terms % 2 * TILE
                for s in range(count):
                    dones[mode][target, s, term, low_row - start : high_row - start, :] = middle[
                        low_row - shift : high_row - shift, s * TILE : (s + 1) * TILE
                    ]
        for mode, (turned, _, _) in enumerate(modes):
            if not turned:
                out_copy(mode, trip * 2).start()
                out_copy(mode, trip * 2 + 1).start()

    for mode, (turned, _, _) in enumerate(modes):
        if turned:
            for block in range(8):
                out_copy(mode, block).start()
    for mode in range(len(modes)):
        for block in range(8):
            out_copy(mode, block).wait()


def left_stage(pieces, plan, modes, count, left_blocks, place, pairs, size, first_sector):
    terms = left_blocks.shape[0]
    blocks = [(count, terms, length, TILE) for _, _, length in modes]
    shapes = []
    for (turned, _, _), block in zip(modes, blocks):
        shapes += [block] * 8 if turned else [(8, *block)]
    anywhere = pl.BlockSpec(memory_space=pl.ANY)
    results = pl.pallas_call(
        functools.partial(left_kernel, first_sector, modes, plan),
        out_shape=[jax.ShapeDtypeStruct(shape, BF16) for shape in shapes],
        grid_spec=pltpu.PrefetchScalarGridSpec(
            num_scalar_prefetch=3,
            grid=(1,),
            in_specs=[anywhere] * (len(pieces) + 1),
            out_specs=[anywhere] * len(shapes),
            scratch_shapes=[
                pltpu.VMEM((count, 64, TILE, TILE), BF16),
                pltpu.VMEM(left_blocks.shape, BF16),
                pltpu.SemaphoreType.DMA((32,)),
                pltpu.SemaphoreType.DMA((4,)),
                pltpu.SemaphoreType.DMA((len(modes), 8)),
            ]
            + [pltpu.VMEM((8, *block), BF16) for block in blocks],
        ),
        compiler_params=pltpu.CompilerParams(vmem_limit_bytes=60 << 20),
        cost_estimate=pl.CostEstimate(
            flops=2 * terms * 2048 * 256 * count * TILE,
            bytes_accessed=(2 << 20) + (terms * 2048 + 8192) * count * TILE * 2,
            transcendentals=0,
        ),
    )(place, pairs, size, *pieces, left_blocks)
    results = list(results)
    return [[results.pop(0) for _ in range(8 if turned else 1)] for turned, _, _ in modes]


def exchange(blocks):
    if len(blocks) == 1:
        return [lax.all_to_all(blocks[0], "bond", split_axis=0, concat_axis=0, tiled=True)]
    got = [blocks[0]]
    for turned in range(1, 8):
        step_x, step_core = turned // 2, turned % 2
        pairs = [
            (x * 2 + core, (x + step_x) % SIDE * 2 + (core + step_core) % 2)
            for x in range(SIDE)
            for core in range(2)
        ]
        got.append(lax.ppermute(blocks[turned], "bond", pairs))
    return got


def right_kernel(layout, half, place, pairs, size, *refs):
    total = sum(8 if turned else 1 for _, turned in layout)
    arrived, right = list(refs[:total]), refs[total]
    rest = refs[total + 1 :]
    if half == 0:
        outs_a, outs_b, rest = rest[:4], rest[4:8], rest[8:]
    else:
        out, rest = rest[0], rest[1:]
    middle, blocks, sum_a, sum_b, sems, right_sems, out_sems = rest
    first_row = sum(SPLIT[:half])
    bond = place[2]
    rows, terms = middle.shape[2], middle.shape[1]
    copies = []
    first = 0
    for count, turned in layout:
        whole = None if turned else arrived.pop(0)
        for block in range(8):
            source = block
            piece = arrived.pop(0) if turned else whole.at[block]
            if turned:
                source = (bond // 2 + SIDE - block // 2) % SIDE * 2 + (bond + block) % 2
            if piece.shape[2] != rows:
                piece = piece.at[:, :, first_row : first_row + rows]
            copies.append(
                pltpu.make_async_copy(
                    piece, middle.at[pl.ds(source * 8 + first, count)], sems.at[len(copies)]
                )
            )
        first += count
    for copy in copies:
        copy.start()

    def owner_of(step_z, step_y):
        return (place[0] + step_y) % SIDE * SIDE + (place[1] + step_z) % SIDE

    def right_copy(step_z, step_y):
        return pltpu.make_async_copy(
            right.at[:, pl.ds(owner_of(step_z, step_y) * 4, 4)],
            blocks.at[step_z * SIDE + step_y],
            right_sems.at[step_z * SIDE + step_y],
        )

    for step_y in range(SIDE):
        right_copy(0, step_y).start()
    lane = lax.broadcasted_iota(jnp.int32, (rows, TILE), 1)
    lives = []
    for h in range(2):
        low, high = max(first_row, h * TILE), min(first_row + rows, (h + 1) * TILE)
        if low < high:
            line = lax.broadcasted_iota(jnp.int32, (high - low, TILE), 0) + (low - h * TILE)
            lives.append(line < size[bond * 2 + h])
    row_live = jnp.concatenate(lives, axis=0)
    for batch, step_zs in enumerate(((1,), (2, 3))):
        for copy in copies[batch * 16 : batch * 16 + 16]:
            copy.wait()
        for step_z in step_zs:
            for step_y in range(SIDE):
                right_copy(step_z, step_y).start()
    sent = []
    for step_zs in ((0, 1), (2, 3)):

        @pl.loop(0, SIDE)
        def _(trip):
            step_z, pair = step_zs[0] + trip // 2, trip % 2 * 2
            for step_y in (pair, pair + 1):
                right_copy(step_z, step_y).wait()
            for step_y in (pair, pair + 1):
                owner = owner_of(step_z, step_y)
                block = blocks.at[step_z * SIDE + step_y]
                for q in range(4):
                    col = owner * 4 + q
                    lhs = jnp.concatenate(
                        [
                            middle[pairs[(term * 64 + col) * 2 + p], term]
                            for term in range(terms)
                            for p in range(2)
                        ],
                        axis=1,
                    )
                    rhs = jnp.concatenate(
                        [block[term, q, p] for term in range(terms) for p in range(2)], axis=0
                    )
                    product = jnp.dot(lhs, rhs, preferred_element_type=F32)
                    keep = row_live & (lane < size[col])
                    value = jnp.where(keep, product, 0.0).astype(BF16)
                    if half == 1:
                        sum_a[owner, :, q * TILE : (q + 1) * TILE] = value
                    elif q < 2:
                        sum_a[step_z, step_y, :, q * TILE : (q + 1) * TILE] = value
                    else:
                        sum_b[step_y, step_z, :, (q - 2) * TILE : (q - 1) * TILE] = value

        for step_z in step_zs if half == 0 else ():
            sent.append(
                pltpu.make_async_copy(sum_a.at[step_z], outs_a[step_z], out_sems.at[len(sent)])
            )
            sent[-1].start()
            for k in range(SIDE):
                sent.append(
                    pltpu.make_async_copy(
                        sum_b.at[k, step_z], outs_b[k].at[step_z], out_sems.at[len(sent)]
                    )
                )
                sent[-1].start()
    if half == 1:
        sent.append(pltpu.make_async_copy(sum_a, out, out_sems.at[0]))
        sent[-1].start()
    for copy in sent:
        copy.wait()


def right_stage(arrived, half, right_blocks, place, pairs, size):
    layout = tuple((count, len(blocks) > 1) for count, blocks in zip(CHUNKS, arrived))
    arrived = [block for blocks in arrived for block in blocks]
    terms, rows = right_blocks.shape[0], SPLIT[half]
    if half == 0:
        shapes = [jax.ShapeDtypeStruct((SIDE, rows, 2 * TILE), BF16)] * 8
        scratch = [pltpu.VMEM((SIDE, SIDE, rows, 2 * TILE), BF16)] * 2
    else:
        shapes = [jax.ShapeDtypeStruct((GROUP, rows, 4 * TILE), BF16)]
        scratch = [pltpu.VMEM(shapes[0].shape, BF16), pltpu.VMEM((16, TILE), BF16)]
    anywhere = pl.BlockSpec(memory_space=pl.ANY)
    return pl.pallas_call(
        functools.partial(right_kernel, layout, half),
        out_shape=shapes,
        grid_spec=pltpu.PrefetchScalarGridSpec(
            num_scalar_prefetch=3,
            grid=(1,),
            in_specs=[anywhere] * (len(arrived) + 1),
            out_specs=[anywhere] * len(shapes),
            scratch_shapes=[
                pltpu.VMEM((64, terms, rows, TILE), BF16),
                pltpu.VMEM((GROUP, terms, 4, 2, TILE, TILE), BF16),
                *scratch,
                pltpu.SemaphoreType.DMA((8 * len(layout),)),
                pltpu.SemaphoreType.DMA((GROUP,)),
                pltpu.SemaphoreType.DMA((SIDE * (SIDE + 1),)),
            ],
        ),
        compiler_params=pltpu.CompilerParams(vmem_limit_bytes=58 << 20),
        cost_estimate=pl.CostEstimate(
            flops=2 * terms * rows * 256 * 8192,
            bytes_accessed=(14 << 20),
            transcendentals=0,
        ),
    )(place, pairs, size, *arrived, right_blocks)


def sum_kernel(*refs):
    inputs, outputs = refs[:8], refs[8:]
    for half in range(2):
        mine = inputs[half * 4 : half * 4 + 4]
        total = mine[0][...].astype(F32)
        for other in mine[1:]:
            total = total + other[...].astype(F32)
        kept = outputs[half * 4 : half * 4 + 4]
        for k in range(SIDE):
            kept[k][...] = total[k].astype(BF16)


def sum_stage(pieces):
    rows, width = pieces[0].shape[1:]
    whole = pl.BlockSpec(memory_space=pltpu.VMEM)
    return pl.pallas_call(
        sum_kernel,
        name="near_sum",
        out_shape=[jax.ShapeDtypeStruct((rows, width), BF16)] * 8,
        in_specs=[whole] * 8,
        out_specs=[whole] * 8,
        compiler_params=pltpu.CompilerParams(vmem_limit_bytes=16 << 20),
    )(*pieces)


def last_kernel(*refs):
    block, out = refs[-2], refs[-1]
    rows, width = refs[0].shape
    for side in range(2):
        mine = refs[side * 4 : side * 4 + 4]
        total = mine[0][...].astype(F32)
        for other in mine[1:]:
            total = total + other[...].astype(F32)
        out[:rows, side * width : (side + 1) * width] = total
    total = block[0].astype(F32)
    for source in range(1, GROUP):
        total = total + block[source].astype(F32)
    out[rows:, :] = total


def last_stage(pieces):
    rows, width = sum(SPLIT), 4 * TILE
    whole = pl.BlockSpec(memory_space=pltpu.VMEM)
    return pl.pallas_call(
        last_kernel,
        name="far_sum",
        out_shape=jax.ShapeDtypeStruct((rows, width), F32),
        in_specs=[whole] * len(pieces),
        out_specs=whole,
        compiler_params=pltpu.CompilerParams(vmem_limit_bytes=16 << 20),
    )(*pieces)


def turn(value, d, along_y):
    return move(value, d, 0) if along_y else move(value, 0, d)


def apply_slab(wave_slab, left_blocks, right_blocks, sector_size, left_pairs, right_pairs):
    group = lax.axis_index("op")
    place = jnp.stack([group // SIDE, group % SIDE, lax.axis_index("bond")]).astype(jnp.int32)
    lefts, rights = left_pairs.reshape(-1), right_pairs.reshape(-1)
    chunk_count = len(CHUNKS)
    starts = [sum(CHUNKS[:chunk]) for chunk in range(chunk_count + 1)]
    wave = wave_slab.reshape(4, TILE, wave_slab.shape[1])
    ahead = min(2, chunk_count)

    def sent_both(values, y_first):
        return [
            [value] + [turn(value, d, (side == 0) == y_first) for d in range(1, SIDE)]
            for side, value in enumerate(values)
        ]

    units = range(starts[ahead])
    values = pack_stage(wave, [], [[(None, side, unit) for unit in units] for side in range(2)])
    got = sent_both(values, False)
    first = sent_both(values, True)
    near = {chunk: ([got[0][1:], got[1][1:]], starts[chunk]) for chunk in range(ahead)}
    arrived = []
    for chunk in range(chunk_count):
        count = CHUNKS[chunk]
        after = chunk + ahead
        sources, offset = near[chunk]
        early = chunk < ahead
        packs = []
        for side in range(2):
            pack = []
            if not early:
                pack += [(None, side, starts[chunk] + unit) for unit in range(count)]
            for d in range(SIDE - 1):
                pack += [(side * 3 + d, side, offset + unit) for unit in range(count)]
            if after < chunk_count:
                pack += [(None, 1 - side, starts[after] + unit) for unit in range(CHUNKS[after])]
            packs.append(pack)
        values = pack_stage(wave, sources[0] + sources[1], packs)
        got = sent_both(values, True)
        pieces, plan = [], []
        for side in range(2):
            for far in range(SIDE):
                slots = range(1, SIDE) if early else range(SIDE)
                plan += [
                    (len(pieces), place_of * count, side, far, slot)
                    for place_of, slot in enumerate(slots)
                ]
                pieces.append(got[side][far])
                if early:
                    plan.append((len(pieces), starts[chunk], side, far, 0))
                    pieces.append(first[side][far])
        if after < chunk_count:
            skip = (SIDE - 1 if early else SIDE) * count
            near[after] = ([got[1][1:], got[0][1:]], skip)
        middles = left_stage(
            pieces,
            tuple(plan),
            MODES[chunk],
            count,
            left_blocks,
            place,
            lefts,
            sector_size,
            starts[chunk],
        )
        for middle in middles:
            arrived.append(exchange(middle))
    parts = []
    for half in range(2):
        mine = arrived[: chunk_count - 1] + [arrived[chunk_count - 1 + half]]
        parts.append(right_stage(mine, half, right_blocks, place, rights, sector_size))
    block = lax.all_to_all(parts[1][0], "op", split_axis=0, concat_axis=0, tiled=True)
    parts = parts[0]
    got = [parts[0]] + [move(parts[d], 0, d) for d in range(1, SIDE)]
    got += [parts[4]] + [move(parts[4 + d], d, 0) for d in range(1, SIDE)]
    sums = sum_stage(got)
    finals = [sums[0]] + [move(sums[d], d, 0) for d in range(1, SIDE)]
    finals += [sums[4]] + [move(sums[4 + d], 0, d) for d in range(1, SIDE)]
    finals.append(block)
    return last_stage(finals)


def solution(mesh):
    placed = (
        P("op", "bond"),
        P("op", None, None, None, None),
        P("op", None, None, None, None),
        P(),
        P("op", None, None),
        P("op", None, None),
    )
    return jax.shard_map(
        apply_slab, mesh=mesh, in_specs=placed, out_specs=P("bond", "op"), check_vma=False
    )
```
